128 devices in a mesh: clip: 2 (over core), tm: 16 (over z, x), head: 4 (over y).
Axes of the slice: x: 4, y: 4, z: 4, core: 2. Of those that a mesh axis runs over, the one named last changes fastest.
Arguments:
- video_tokens: bfloat16 [64, 1568, 1024], P(('clip', 'tm')), parts along dimension 0, may hold values from -6 to 6
- window_order: int32 [64, 1568], P(('clip', 'tm')), parts along dimension 0, may hold values from 0 to 1567, each once within a row
- clip_id: int32 [64], P(('clip', 'tm')), parts along dimension 0, may hold values from 0 to 7, never falling along the last dimension, each value on 1 to 8 neighbouring positions
- attend_weight: bfloat16 [3, 1024, 1024], P(None, None, 'head'), may hold values from -0.75 to 0.75
- attend_out: bfloat16 [1024, 1024], P('head'), may hold values from -0.1875 to 0.1875
- recur_weight: bfloat16 [3, 1024, 1024], P(None, None, 'head'), may hold values from -0.1875 to 0.1875
- frame_decay: float32 [64, 1024], P(('clip', 'tm'), 'head'), parts along dimension 0, may hold values from -5.7 to -0.010625, as said below
- recur_out: bfloat16 [1024, 1024], P('head'), may hold values from -0.1875 to 0.1875
Outputs:
- features_out: bfloat16 [64, 1568, 1024], P(('clip', 'tm'), None, 'head'), parts along dimension 0
The draws below stay inside these ranges and needn't reach their ends.
There are 2 independent parts, one for each index of `clip`. The reference program is written for one: setup_inputs(seed, part) draws one part's arguments, and reference() takes and returns one part's arrays. A program takes and returns all parts, laid end to end along the dimension named above; an argument that names none is the same for every part. Nothing has to cross between parts.
Inputs may be any that keep to these rules, and one draw needn't show every extreme that they name: `clip_id`: never falls along the frames; a clip spans 1 to 8 frames. `frame_decay`: negative.
All inputs are finite; a program needn't handle non-finite values.
Results may differ from the reference program's by a relative error of at most 0.01.
Values may be sent and summed in bfloat16 or wider, within the bound.
No kernel may reach another device: no remote copies, remote signals or barrier semaphores. Data moves between devices by JAX's collectives and lax.ppermute only.
A program may use at most 128 MiB of HBM per device.

```python
import math
import jax
import jax.numpy as jnp
import numpy as np
from jax import lax

HEAD_DIMENSION = 64
WINDOW = 49
MODEL_DIMENSION = 1024
F_DEV = 2
TOKF = 1568
FRAME_TOTAL = 32
N_TM = 16
N_HEAD = 4


def draw_attend_weight(key, part):
    first_key, second_key, third_key = jax.random.split(jax.random.fold_in(key, 11), 3)
    shared = jnp.clip(jax.random.normal(first_key, (MODEL_DIMENSION, MODEL_DIMENSION), jnp.float32), -4.0, 4.0)
    random_perturbation = jnp.clip(jax.random.normal(second_key, (MODEL_DIMENSION, MODEL_DIMENSION), jnp.float32), -4.0, 4.0)
    value_part = jnp.clip(jax.random.normal(third_key, (MODEL_DIMENSION, MODEL_DIMENSION), jnp.float32), -4.0, 4.0)
    query_part = shared
    key_part = random_perturbation
    return (jnp.stack([query_part, key_part, value_part]) / jnp.sqrt(jnp.float32(MODEL_DIMENSION))).astype(jnp.bfloat16)


def draw_frame_decay(key, part):
    random_child_keys = jax.random.split(jax.random.fold_in(key, 23), 6)
    number_of_heads = MODEL_DIMENSION // HEAD_DIMENSION
    slow_share = 0.5
    slow_head = jax.random.uniform(random_child_keys[0], (number_of_heads,)) < slow_share
    slow_channel = jnp.repeat(slow_head, HEAD_DIMENSION)
    fast_rate = jnp.exp(jax.random.uniform(random_child_keys[1], (MODEL_DIMENSION,), jnp.float32, jnp.log(0.7), jnp.log(2.5)))
    slow_rate = jax.random.uniform(random_child_keys[2], (MODEL_DIMENSION,), jnp.float32, 0.3, 1.0) * 2.3 / FRAME_TOTAL
    default_decay_rate = jnp.where(slow_channel, slow_rate, fast_rate)
    random_perturbation = jnp.exp(jax.random.uniform(random_child_keys[3], (FRAME_TOTAL, MODEL_DIMENSION), jnp.float32, jnp.log(0.5), jnp.log(2.0)))
    spike_head_index = jax.random.uniform(random_child_keys[4], (FRAME_TOTAL, number_of_heads)) < 3.0 / FRAME_TOTAL
    spike_regions = jnp.repeat(spike_head_index, HEAD_DIMENSION, axis=1)
    spike_length = jax.random.uniform(random_child_keys[5], (FRAME_TOTAL, MODEL_DIMENSION), jnp.float32, 0.22, 0.69)
    return -(default_decay_rate[None, :] * random_perturbation + jnp.where(spike_regions, spike_length, 0.0))


def block_scale(key, shape, shards, smallest, top_value):
    def one(position, shards_of):
        draws = jax.random.uniform(jax.random.fold_in(jax.random.fold_in(key, 6), position), (shards_of,), jnp.float32, smallest / len(shards), top_value / len(shards))
        return jnp.repeat(jnp.exp(draws), shape[position] // shards_of).reshape((-1,) + (1,) * (len(shape) - position - 1))

    level = one(*shards[0])
    for cut in shards[1:]:
        level = level * one(*cut)
    return level


def length_profile(number_of, total, limit, lean):
    weights = [(1 << 20) // math.isqrt(grade ** lean) + 1 for grade in range(2, number_of + 1)]
    rest, holding = total - limit - (number_of - 1), [1] * (number_of - 1)
    while rest > 0:
        free = [i for i in range(number_of - 1) if holding[i] < limit]
        pool, left = sum([weights[i] for i in free]), rest
        for i in free:
            addition = min(limit - holding[i], max(1, left * weights[i] // pool), rest)
            holding[i] = holding[i] + addition
            rest = rest - addition
    return np.array([limit] + holding)


def ragged(rng, count, total, limit, lean):
    if count == 2:
        one = jax.random.randint(rng, (), max(1, total - limit), min(limit, total - 1) + 1)
        return jnp.stack([one, total - one])
    sizes = jnp.asarray(length_profile(count, total, limit, lean), jnp.int32)
    couples = (count - 1) // 2
    donor, taker = sizes[1:1 + 2 * couples:2], sizes[2:2 + 2 * couples:2]
    room = jnp.minimum(donor - 1, limit - taker)
    shifted = jax.random.randint(jax.random.fold_in(rng, 1), (couples,), 0, 1 << 20) % (room + 1)
    sizes = sizes.at[1:1 + 2 * couples:2].set(donor - shifted).at[2:2 + 2 * couples:2].set(taker + shifted)
    return sizes[jax.random.permutation(jax.random.fold_in(rng, 2), count)]


def scatter_about(own_key, shape, deviation, bound, cuts=(), kind=jnp.bfloat16):
    entries = deviation * jax.random.normal(own_key, shape, jnp.float32)
    if cuts:
        entries = entries * block_scale(own_key, shape, cuts, -0.22, 0.18)
    return jnp.clip(entries, -bound, bound).astype(kind)


def setup_inputs(seed: int = 0, part: int = 0) -> dict:
    splits = jax.random.split(jax.random.key(seed), 9)
    part_splits = jax.random.split(jax.random.fold_in(splits[8], part), 9)
    return {
        "video_tokens": scatter_about(part_splits[0], (FRAME_TOTAL, TOKF, MODEL_DIMENSION), 1.0, 6.0, ((0, 16),)),
        "window_order": jax.vmap(lambda own: jax.random.permutation(own, TOKF))(jax.random.split(part_splits[1], FRAME_TOTAL)).reshape((FRAME_TOTAL, TOKF)).astype(jnp.int32),
        "clip_id": jnp.searchsorted(jnp.cumsum(ragged(part_splits[2], N_TM // 2, FRAME_TOTAL, 4 * F_DEV, 1)), jnp.arange(FRAME_TOTAL), side="right").astype(jnp.int32),
        "attend_weight": draw_attend_weight(jax.random.fold_in(splits[8], 71), part),
        "attend_out": scatter_about(splits[4], (MODEL_DIMENSION, MODEL_DIMENSION), MODEL_DIMENSION ** -0.5, 0.1875, ((0, 4),)),
        "recur_weight": scatter_about(splits[5], (3, MODEL_DIMENSION, MODEL_DIMENSION), MODEL_DIMENSION ** -0.5, 0.1875, ((2, 4),)),
        "frame_decay": draw_frame_decay(jax.random.fold_in(jax.random.fold_in(splits[8], part), 71), part),
        "recur_out": scatter_about(splits[7], (MODEL_DIMENSION, MODEL_DIMENSION), MODEL_DIMENSION ** -0.5, 0.1875, ((0, 4),)),
    }


EPSILON = 1e-06

def normalize(values):
    return values * lax.rsqrt(lax.optimization_barrier(jnp.mean(values * values, axis=-1, keepdims=True)) + EPSILON)

def window_attention(queries, keys_all, values_all, window_order):
    frame_count, positions, number_of_heads, head_size = queries.shape
    order_index = window_order.astype(jnp.int32)[:, :, None, None]

    def arrange(tensor):
        reordered = jnp.take_along_axis(tensor, order_index, axis=1)
        return reordered.reshape(frame_count, positions // WINDOW, WINDOW, number_of_heads, head_size).astype(jnp.float32)
    scores = jnp.einsum('fwihe,fwjhe->fwhij', arrange(queries), arrange(keys_all)) / jnp.sqrt(jnp.float32(head_size))
    weights = jax.nn.softmax(scores, axis=-1).astype(jnp.bfloat16)
    blended = jnp.einsum('fwhij,fwjhe->fwihe', weights.astype(jnp.float32), arrange(values_all)).astype(jnp.bfloat16)
    blended = blended.reshape(frame_count, positions, number_of_heads, head_size)
    inverse = jnp.argsort(window_order, axis=1).astype(jnp.int32)
    return jnp.take_along_axis(blended, inverse[:, :, None, None], axis=1)

def grouped_product(left_side, right_side):
    group_width = left_side.shape[1] // N_HEAD
    running = jnp.zeros((left_side.shape[0], right_side.shape[1]), jnp.float32)
    for member in range(N_HEAD):
        partial_term = jnp.dot(left_side[:, member * group_width:(member + 1) * group_width], right_side[member * group_width:(member + 1) * group_width], preferred_element_type=jnp.float32)
        rounded = lax.optimization_barrier(partial_term.astype(jnp.bfloat16))
        running = running + rounded.astype(jnp.float32)
    return running

def reference(video_tokens, window_order, clip_id, attend_weight, attend_out, recur_weight, frame_decay, recur_out):
    frame_count, positions, model_width = video_tokens.shape
    number_of_heads = model_width // HEAD_DIMENSION
    inputs = video_tokens.astype(jnp.float32).reshape(-1, model_width)
    normed = normalize(inputs).astype(jnp.bfloat16)
    projected = jnp.einsum('td,kde->kte', normed.astype(jnp.float32), attend_weight.astype(jnp.float32)).astype(jnp.bfloat16)
    shaped = projected.reshape(3, frame_count, positions, number_of_heads, HEAD_DIMENSION)
    attended = window_attention(shaped[0], shaped[1], shaped[2], window_order).reshape(-1, model_width)
    residual = inputs + grouped_product(attended, attend_out)
    normed_again = normalize(residual).astype(jnp.bfloat16)
    recur_proj = jnp.einsum('td,kde->kte', normed_again.astype(jnp.float32), recur_weight.astype(jnp.float32))
    gate_in = jax.nn.sigmoid(recur_proj[0]).reshape(frame_count, positions, model_width)
    value_in = recur_proj[1].reshape(frame_count, positions, model_width)
    out_gate = jax.nn.silu(recur_proj[2]).reshape(frame_count, positions, model_width)
    retain = jnp.exp(frame_decay)
    driven = jnp.sqrt(1.0 - retain * retain)[:, None, :] * gate_in * value_in
    continues = jnp.concatenate([jnp.zeros((1,), jnp.float32), (clip_id[1:] == clip_id[:-1]).astype(jnp.float32)])
    factor = retain * continues[:, None]

    def advance(state_now, inputs_now):
        factor_now, driven_now = inputs_now
        state_now = factor_now[None, :] * state_now + driven_now
        return (state_now, state_now)
    final_state, states = lax.scan(advance, jnp.zeros((positions, model_width), jnp.float32), (factor, driven))
    output_rows = (states * out_gate).astype(jnp.bfloat16).reshape(-1, model_width)
    result = residual + grouped_product(output_rows, recur_out)
    return result.astype(jnp.bfloat16).reshape(frame_count, positions, model_width)
```

```python
import functools
import jax
import jax.numpy as jnp
from jax import lax
from jax.experimental import pallas as pl
from jax.experimental.pallas import tpu as pltpu
from jax.sharding import Mesh, PartitionSpec as P

HEAD = 64
WINDOW = 49
SLOT = 64
TOK = 1568
WINDOWS = TOK // WINDOW
ROWS = WINDOWS * SLOT
D = 1024
C = 256
FRAMES = 2
QUARTER = TOK // 4
STRIDE = 96
SHARE = 104
SENT = SHARE + 8
EPSILON = 1e-06
F32 = jnp.float32
BF16 = jnp.bfloat16
LIMIT = 60 * 1024 * 1024


def dot(left, right):
    return jnp.dot(left, right, preferred_element_type=F32)


def dot_t(left, right):
    return lax.dot_general(left, right, (((1,), (1,)), ((), ())), preferred_element_type=F32)


def scaled(values):
    return values * lax.rsqrt(jnp.mean(values * values, axis=-1, keepdims=True) + EPSILON)


def attend_kernel(x_ref, column_ref, row_ref, decay_ref, continues_ref, weight_ref, out_ref, normed, qkv, arranged, mixed):
    step = 112

    def norm_step(i, carry):
        rows = pl.ds(pl.multiple_of(i * step, 16), step)
        normed[rows, :] = scaled(x_ref[0, rows, :].astype(F32)).astype(BF16)
        return carry

    lax.fori_loop(0, TOK // step, norm_step, 0)

    half = TOK // 2
    for i in range(2):
        for k in range(3):
            rows = slice(i * half, (i + 1) * half)
            qkv[rows, k * C : (k + 1) * C] = dot(normed[rows, :], weight_ref[k]).astype(BF16)

    part = 512

    def arrange_step(i, carry):
        rows = pl.ds(pl.multiple_of(i * part, part), part)
        lanes = lax.broadcasted_iota(jnp.int32, (part, TOK), 1)
        pick = jnp.where(lanes == column_ref[0, rows, :], 1.0, 0.0).astype(BF16)
        arranged[rows, :] = dot(pick, qkv[...]).astype(BF16)
        return carry

    lax.fori_loop(0, ROWS // part, arrange_step, 0)

    lane_head = lax.broadcasted_iota(jnp.int32, (SLOT, C), 1) // HEAD
    own = [lane_head == h for h in range(4)]
    row_index = lax.broadcasted_iota(jnp.int32, (C, C), 0)
    lane_index = lax.broadcasted_iota(jnp.int32, (C, C), 1)
    together = jnp.where(row_index // HEAD == lane_index // HEAD, 1.0, 0.0).astype(BF16)
    group = 4
    lane = lax.broadcasted_iota(jnp.int32, (group * SLOT, 128), 1)
    low = lane < SLOT
    valid = (lane % SLOT) < WINDOW
    floor = -3.0e38

    def spread(block):
        return jnp.concatenate([jnp.where(own[h], block, jnp.zeros_like(block)) for h in range(4)], axis=0)

    def window_step(i, carry):
        base = i * (group * SLOT)
        scores = []
        for w in range(group):
            rows = pl.ds(pl.multiple_of(base + w * SLOT, SLOT), SLOT)
            scores.append(dot_t(arranged[rows, 0:C], spread(arranged[rows, C : 2 * C])))
        scores = jnp.concatenate(scores, axis=0) * 0.125
        pieces = []
        for side in range(2):
            piece = jnp.where(valid, scores[:, side * 128 : (side + 1) * 128], floor)
            top_low = jnp.max(jnp.where(low, piece, floor), axis=-1, keepdims=True)
            top_high = jnp.max(jnp.where(low, floor, piece), axis=-1, keepdims=True)
            pieces.append(jnp.exp(piece - jnp.where(low, top_low, top_high)))
        weights = jnp.concatenate(pieces, axis=1).astype(BF16)
        totals = dot(weights, together)
        blended = []
        for w in range(group):
            rows = pl.ds(pl.multiple_of(base + w * SLOT, SLOT), SLOT)
            blended.append(dot(weights[w * SLOT : (w + 1) * SLOT], spread(arranged[rows, 2 * C : 3 * C])))
        blended = jnp.concatenate(blended, axis=0) / totals
        mixed[pl.ds(pl.multiple_of(base, group * SLOT), group * SLOT), :] = blended.astype(BF16)
        return carry

    lax.fori_loop(0, WINDOWS // group, window_step, 0)

    decay = decay_ref[0]
    high = decay.astype(BF16).astype(F32)
    middle = (decay - high).astype(BF16).astype(F32)
    index = lax.broadcasted_iota(jnp.int32, (8, C), 0)
    extra = jnp.where(
        index == 0,
        high,
        jnp.where(index == 1, middle, jnp.where(index == 2, (decay - high) - middle, continues_ref[0])),
    ).astype(BF16)

    def restore_step(i, carry):
        r = lax.broadcasted_iota(jnp.int32, (4 * SHARE, ROWS), 0)
        late = jnp.where(r >= SHARE, 8, 0) + jnp.where(r >= 2 * SHARE, 8, 0) + jnp.where(r >= 3 * SHARE, 8, 0)
        position = r - late + i * QUARTER
        pick = jnp.where(position == row_ref[0], 1.0, 0.0).astype(BF16)
        result = dot(pick, mixed[...])
        for h in range(4):
            out_ref[4 * i + h, 0, :SHARE, :] = result[h * SHARE : (h + 1) * SHARE].astype(BF16)
            out_ref[4 * i + h, 0, SHARE:, :] = extra
        return carry

    lax.fori_loop(0, 4, restore_step, 0)


def attend(tokens, window_order, frame_decay, continues, weight):
    padded = jnp.pad(
        window_order.reshape(FRAMES, WINDOWS, WINDOW),
        ((0, 0), (0, 0), (0, SLOT - WINDOW)),
        constant_values=-1,
    ).reshape(FRAMES, ROWS)
    return pl.pallas_call(
        attend_kernel,
        grid=(FRAMES,),
        in_specs=[
            pl.BlockSpec((1, TOK, D), lambda f: (f, 0, 0)),
            pl.BlockSpec((1, ROWS, 1), lambda f: (f, 0, 0)),
            pl.BlockSpec((1, 1, ROWS), lambda f: (f, 0, 0)),
            pl.BlockSpec((1, 1, C), lambda f: (f, 0, 0)),
            pl.BlockSpec((1, 1, C), lambda f: (f, 0, 0)),
            pl.BlockSpec((3, D, C), lambda f: (0, 0, 0)),
        ],
        out_specs=pl.BlockSpec((16, 1, SENT, C), lambda f: (0, f, 0, 0)),
        out_shape=jax.ShapeDtypeStruct((16, FRAMES, SENT, C), BF16),
        scratch_shapes=[
            pltpu.VMEM((TOK, D), BF16),
            pltpu.VMEM((TOK, 3 * C), BF16),
            pltpu.VMEM((ROWS, 3 * C), BF16),
            pltpu.VMEM((ROWS, C), BF16),
        ],
        compiler_params=pltpu.CompilerParams(vmem_limit_bytes=LIMIT),
        cost_estimate=pl.CostEstimate(
            flops=2 * FRAMES * (TOK * D * 3 * C + ROWS * TOK * 3 * C + 4 * ROWS * C * C + ROWS * TOK * C),
            bytes_accessed=FRAMES * TOK * D * 4,
            transcendentals=FRAMES * ROWS * C,
        ),
        name="attend",
    )(tokens, padded[:, :, None], padded[:, None, :], frame_decay[:, None, :], continues, weight)


def recur_kernel(
    place_ref, att_ref, x0_ref, x1_ref, x2_ref, x3_ref, mix_ref, gate_ref, value_ref, open_ref,
    residual_ref, state_ref, decay_ref, open_out_ref, last_ref,
    normed,
):
    x = place_ref[0]
    h = pl.program_id(0)
    count = FRAMES * SHARE

    @pl.when(h == 0)
    def _():
        for s, x_ref in enumerate((x0_ref, x1_ref, x2_ref, x3_ref)):
            source = lax.rem(x + (4 - s), 4)
            pieces = []
            for c in range(2):
                for q in range(2):
                    total = None
                    for k in range(4):
                        left = att_ref[4 * source + k, :, :SHARE, :].reshape(count, C)
                        term = dot(left, mix_ref[c, k, q * C : (q + 1) * C, :])
                        total = term if total is None else total + term
                    pieces.append(total)
            residual = x_ref[...].reshape(count, D).astype(F32) + jnp.concatenate(pieces, axis=1)
            residual_ref[source] = residual
            normed[source] = scaled(residual).astype(BF16)

    rows = normed[...].reshape(4 * count, D)

    def project(ref):
        return dot(rows[:, : D // 2], ref[0, 0]) + dot(rows[:, D // 2 :], ref[1, 0])

    driven = jax.nn.sigmoid(project(gate_ref)) * project(value_ref)
    opening = project(open_ref)
    open_out_ref[0] = opening * jax.nn.sigmoid(opening)
    state = jnp.zeros((SHARE, C), F32)
    decay = jnp.ones((1, C), F32)
    for f in range(4 * FRAMES):
        extra = att_ref[(f // 2) * 4 + h, f % 2, SHARE:, :].astype(F32)
        retain = jnp.exp(extra[0:1] + extra[1:2] + extra[2:3])
        factor = retain * extra[3:4]
        drive = jnp.sqrt(1.0 - retain * retain)
        decay = factor * decay
        state = factor * state + drive * driven[f * SHARE : (f + 1) * SHARE]
        state_ref[0, f * SHARE : (f + 1) * SHARE, :] = state
        decay_ref[0, f : f + 1, :] = decay
    last_ref[0] = state.astype(BF16)


def finish_kernel(state_ref, decay_ref, open_ref, incoming_ref, residual_ref, weight_ref, out_ref, rows):
    n = pl.program_id(0)

    @pl.when(n == 0)
    def _():
        for k in range(4):
            incoming = incoming_ref[k].astype(F32)
            for f in range(4 * FRAMES):
                piece = slice(f * SHARE, (f + 1) * SHARE)
                state = state_ref[k, piece, :] + decay_ref[k, f : f + 1, :] * incoming
                rows[k, piece, :] = (state * open_ref[k, piece, :]).astype(BF16)

    total = residual_ref[...].reshape(8 * SHARE, C)
    for k in range(4):
        total = total + dot(rows[k], weight_ref[0, k])
    out_ref[...] = total.reshape(4, 1, FRAMES, SHARE, C).astype(BF16)


def place_kernel(in_ref, out_ref):
    for k in range(4):
        size = STRIDE if k < 3 else SHARE
        for f in range(FRAMES):
            out_ref[f, 0, k * STRIDE : k * STRIDE + size, :] = in_ref[0, k, f, :size, :]


def per_device(tokens, window_order, clip_id, attend_weight, attend_out, recur_weight, frame_decay, recur_out):
    c, z, x, h = (lax.axis_index(name) for name in ("clip", "z", "x", "head"))

    def column_blocks(weight):
        blocks = weight.reshape(C, 4, C).transpose(1, 0, 2)
        return lax.dynamic_slice_in_dim(blocks, 2 * c, 2, 0).reshape(2 * C, C)

    half = lax.dynamic_slice_in_dim(recur_weight, c * (D // 2), D // 2, 1).reshape(3 * D // 2, C)
    packed = jnp.concatenate([column_blocks(attend_out), half, column_blocks(recur_out)], axis=0)
    before = lax.ppermute(clip_id[1:], ("z", "x"), [(i, i + 1) for i in range(15)])
    continues = (clip_id == jnp.concatenate([before, clip_id[:1]])).astype(F32)
    continues = continues * jnp.where((jnp.arange(FRAMES) > 0) | (z > 0) | (x > 0), 1.0, 0.0)
    continues = jnp.broadcast_to(continues[:, None, None], (FRAMES, 1, C))
    weights = lax.all_gather(packed, ("clip", "head"), axis=0).reshape(2, 4, 5 * D // 2, C)

    quarters = tokens.reshape(FRAMES, 4, QUARTER, D)
    moved = []
    for s in range(4):
        block = lax.dynamic_slice(
            quarters, (0, lax.rem(x + s, 4), h * STRIDE, 0), (FRAMES, 1, SHARE, D)
        ).reshape(FRAMES, SHARE, D)
        if s:
            block = lax.ppermute(block, "x", [(i, (i + s) % 4) for i in range(4)])
        moved.append(block)

    mixed = attend(tokens, window_order, frame_decay, continues, attend_weight)
    mixed = lax.all_to_all(mixed, ("x", "head"), 0, 0)

    whole = lambda shape: pl.BlockSpec(shape, lambda n: (0,) * len(shape))
    span = D // 2
    wide = 8 * SHARE
    residual, state, decay, opened, last = pl.pallas_call(
        recur_kernel,
        grid=(4,),
        in_specs=[
            pl.BlockSpec(memory_space=pltpu.SMEM),
            whole((16, FRAMES, SENT, C)),
            whole((FRAMES, SHARE, D)),
            whole((FRAMES, SHARE, D)),
            whole((FRAMES, SHARE, D)),
            whole((FRAMES, SHARE, D)),
            pl.BlockSpec((2, 4, span, C), lambda n: (0, 0, 0, 0)),
            pl.BlockSpec((2, 1, span, C), lambda n: (0, n, 1, 0)),
            pl.BlockSpec((2, 1, span, C), lambda n: (0, n, 2, 0)),
            pl.BlockSpec((2, 1, span, C), lambda n: (0, n, 3, 0)),
        ],
        out_specs=[
            whole((4, FRAMES * SHARE, D)),
            pl.BlockSpec((1, wide, C), lambda n: (n, 0, 0)),
            pl.BlockSpec((1, 8, C), lambda n: (n, 0, 0)),
            pl.BlockSpec((1, wide, C), lambda n: (n, 0, 0)),
            pl.BlockSpec((1, SHARE, C), lambda n: (n, 0, 0)),
        ],
        out_shape=[
            jax.ShapeDtypeStruct((4, FRAMES * SHARE, D), F32),
            jax.ShapeDtypeStruct((4, wide, C), F32),
            jax.ShapeDtypeStruct((4, 8, C), F32),
            jax.ShapeDtypeStruct((4, wide, C), F32),
            jax.ShapeDtypeStruct((4, SHARE, C), BF16),
        ],
        scratch_shapes=[pltpu.VMEM((4, FRAMES * SHARE, D), BF16)],
        compiler_params=pltpu.CompilerParams(vmem_limit_bytes=LIMIT),
        name="recur",
    )(x[None], mixed, *moved, weights, weights, weights, weights)

    incoming = lax.ppermute(last, "z", [(i, i + 1) for i in range(3)])

    result = pl.pallas_call(
        finish_kernel,
        grid=(4,),
        in_specs=[
            whole((4, wide, C)),
            whole((4, 8, C)),
            whole((4, wide, C)),
            whole((4, SHARE, C)),
            pl.BlockSpec((4, FRAMES * SHARE, C), lambda n: (0, 0, n)),
            pl.BlockSpec((1, 4, C, C), lambda n: (n // 2, 0, 8 + n % 2, 0)),
        ],
        out_specs=pl.BlockSpec((4, 1, FRAMES, SHARE, C), lambda n: (0, n, 0, 0, 0)),
        out_shape=jax.ShapeDtypeStruct((4, 4, FRAMES, SHARE, C), BF16),
        scratch_shapes=[pltpu.VMEM((4, wide, C), BF16)],
        compiler_params=pltpu.CompilerParams(vmem_limit_bytes=LIMIT),
        name="finish",
    )(state, decay, opened, incoming, residual, weights)

    result = lax.all_to_all(result.reshape(16, FRAMES, SHARE, C), ("x", "head"), 0, 0)
    placed = pl.pallas_call(
        place_kernel,
        grid=(4,),
        in_specs=[pl.BlockSpec((1, 4, FRAMES, SHARE, C), lambda n: (n, 0, 0, 0, 0))],
        out_specs=pl.BlockSpec((FRAMES, 1, QUARTER, C), lambda n: (0, n, 0, 0)),
        out_shape=jax.ShapeDtypeStruct((FRAMES, 4, QUARTER, C), BF16),
        name="place",
    )(result.reshape(4, 4, FRAMES, SHARE, C))
    return placed.reshape(FRAMES, TOK, C)


def solution(mesh):
    split = Mesh(mesh.devices.reshape(2, 4, 4, 4), ("clip", "z", "x", "head"))
    frames = ("clip", "z", "x")
    return jax.shard_map(
        per_device,
        mesh=split,
        in_specs=(
            P(frames, None, None),
            P(frames, None),
            P(frames),
            P(None, None, "head"),
            P("head", None),
            P(None, None, "head"),
            P(frames, "head"),
            P("head", None),
        ),
        out_specs=P(frames, None, "head"),
        check_vma=False,
    )
```

```python
import functools
import jax
import jax.numpy as jnp
from jax import lax
from jax.experimental import pallas as pl
from jax.experimental.pallas import tpu as pltpu
from jax.sharding import Mesh, PartitionSpec as P

HEAD = 64
WINDOW = 49
SLOT = 64
TOK = 1568
WINDOWS = TOK // WINDOW
ROWS = WINDOWS * SLOT
D = 1024
C = 256
FRAMES = 2
QUARTER = TOK // 4
STRIDE = 96
SHARE = 104
SENT = SHARE + 8
EPSILON = 1e-06
F32 = jnp.float32
BF16 = jnp.bfloat16
LIMIT = 40 * 1024 * 1024


def dot(left, right):
    return jnp.dot(left, right, preferred_element_type=F32)


def dot_t(left, right):
    return lax.dot_general(left, right, (((1,), (1,)), ((), ())), preferred_element_type=F32)


def scaled(values):
    return values * lax.rsqrt(jnp.mean(values * values, axis=-1, keepdims=True) + EPSILON)


def pack_kernel(place_ref, tokens_ref, mix_ref, recur_ref, last_ref, packed_ref, *rest):
    block_refs, (packed, blocks, sems, out_sems) = rest[:4], rest[4:]
    c, x, h = place_ref[0], place_ref[1], place_ref[2]
    copies = []

    def copy(source, through, target):
        i = len(copies)
        inward = pltpu.make_async_copy(source, through, sems.at[i])
        copies.append((inward, pltpu.make_async_copy(through, target, out_sems.at[i])))
        inward.start()

    def pack(source, rows):
        copy(source, packed.at[rows, :], packed_ref.at[rows, :])

    for q in range(2):
        columns = pl.ds(pl.multiple_of(c * (2 * C) + q * C, C), C)
        pack(mix_ref.at[:, columns], slice(q * C, (q + 1) * C))
        pack(last_ref.at[:, columns], slice((8 + q) * C, (9 + q) * C))
    for i in range(3):
        half = pl.ds(pl.multiple_of(c * (D // 2), D // 2), D // 2)
        pack(recur_ref.at[i, half, :], slice((i + 1) * D // 2, (i + 2) * D // 2))
    for s, block_ref in enumerate(block_refs):
        part = tokens_ref.at[:, lax.rem(x + s, 4), pl.ds(pl.multiple_of(h * STRIDE, 16), SHARE), :]
        copy(part, blocks.at[s], block_ref)
    for inward, outward in copies:
        inward.wait()
        outward.start()
    for inward, outward in copies:
        outward.wait()


def attend_kernel(x_ref, order_ref, decay_ref, clip_ref, weight_ref, out_ref, normed, qkv, arranged, mixed):
    step = 112

    def norm_step(i, carry):
        rows = pl.ds(pl.multiple_of(i * step, 16), step)
        normed[rows, :] = scaled(x_ref[0, rows, :].astype(F32)).astype(BF16)
        return carry

    lax.fori_loop(0, TOK // step, norm_step, 0)

    half = TOK // 2
    for i in range(2):
        for k in range(3):
            rows = slice(i * half, (i + 1) * half)
            qkv[rows, k * C : (k + 1) * C] = dot(normed[rows, :], weight_ref[k]).astype(BF16)

    lanes = lax.broadcasted_iota(jnp.int32, (128, TOK), 1)
    columns = jnp.transpose(order_ref[0])
    for i in range(ROWS // 512):
        pick = jnp.concatenate(
            [jnp.where(lanes == columns[:, j : j + 1], 1.0, 0.0).astype(BF16) for j in range(4 * i, 4 * i + 4)],
            axis=0,
        )
        arranged[i * 512 : (i + 1) * 512, :] = dot(pick, qkv[...]).astype(BF16)

    lane_head = lax.broadcasted_iota(jnp.int32, (SLOT, C), 1) // HEAD
    own = [lane_head == h for h in range(4)]
    row_index = lax.broadcasted_iota(jnp.int32, (C, C), 0)
    lane_index = lax.broadcasted_iota(jnp.int32, (C, C), 1)
    together = jnp.where(row_index // HEAD == lane_index // HEAD, 1.0, 0.0).astype(BF16)
    group = 4
    lane = lax.broadcasted_iota(jnp.int32, (group * SLOT, 128), 1)
    low = lane < SLOT
    valid = (lane % SLOT) < WINDOW
    floor = -3.0e38

    def spread(block):
        return jnp.concatenate([jnp.where(own[h], block, jnp.zeros_like(block)) for h in range(4)], axis=0)

    def window_step(i, carry):
        base = i * (group * SLOT)
        scores = []
        for w in range(group):
            rows = pl.ds(pl.multiple_of(base + w * SLOT, SLOT), SLOT)
            scores.append(dot_t(arranged[rows, 0:C], spread(arranged[rows, C : 2 * C])))
        scores = jnp.concatenate(scores, axis=0) * 0.125
        pieces = []
        for side in range(2):
            piece = jnp.where(valid, scores[:, side * 128 : (side + 1) * 128], floor)
            top_low = jnp.max(jnp.where(low, piece, floor), axis=-1, keepdims=True)
            top_high = jnp.max(jnp.where(low, floor, piece), axis=-1, keepdims=True)
            pieces.append(jnp.exp(piece - jnp.where(low, top_low, top_high)))
        weights = jnp.concatenate(pieces, axis=1).astype(BF16)
        totals = dot(weights, together)
        blended = []
        for w in range(group):
            rows = pl.ds(pl.multiple_of(base + w * SLOT, SLOT), SLOT)
            blended.append(dot(weights[w * SLOT : (w + 1) * SLOT], spread(arranged[rows, 2 * C : 3 * C])))
        blended = jnp.concatenate(blended, axis=0) / totals
        mixed[pl.ds(pl.multiple_of(base, group * SLOT), group * SLOT), :] = blended.astype(BF16)
        return carry

    lax.fori_loop(0, WINDOWS // group, window_step, 0)

    f = pl.program_id(0)
    decay = decay_ref[pl.ds(f, 1), :]
    clip = clip_ref[f].astype(F32)
    high = decay.astype(BF16).astype(F32)
    middle = (decay - high).astype(BF16).astype(F32)
    index = lax.broadcasted_iota(jnp.int32, (8, C), 0)
    extra = jnp.where(
        index == 0,
        high,
        jnp.where(index == 1, middle, jnp.where(index == 2, (decay - high) - middle, clip)),
    ).astype(BF16)

    def restore_step(i, carry):
        r = lax.broadcasted_iota(jnp.int32, (4 * SHARE, 128), 0)
        late = jnp.where(r >= SHARE, 8, 0) + jnp.where(r >= 2 * SHARE, 8, 0) + jnp.where(r >= 3 * SHARE, 8, 0)
        position = r - late + i * QUARTER
        pick = jnp.concatenate(
            [jnp.where(position == order_ref[0, j : j + 1, :], 1.0, 0.0).astype(BF16) for j in range(ROWS // 128)],
            axis=1,
        )
        result = dot(pick, mixed[...])
        for h in range(4):
            out_ref[4 * i + h, 0, :SHARE, :] = result[h * SHARE : (h + 1) * SHARE].astype(BF16)
            out_ref[4 * i + h, 0, SHARE:, :] = extra
        return carry

    lax.fori_loop(0, 4, restore_step, 0)


def attend(tokens, window_order, frame_decay, clip_id, weight):
    padded = jnp.pad(
        window_order.reshape(FRAMES, WINDOWS, WINDOW),
        ((0, 0), (0, 0), (0, SLOT - WINDOW)),
        constant_values=-1,
    ).reshape(FRAMES, ROWS // 128, 128)
    return pl.pallas_call(
        attend_kernel,
        grid=(FRAMES,),
        in_specs=[
            pl.BlockSpec((1, TOK, D), lambda f: (f, 0, 0)),
            pl.BlockSpec((1, ROWS // 128, 128), lambda f: (f, 0, 0)),
            pl.BlockSpec((FRAMES, C), lambda f: (0, 0)),
            pl.BlockSpec(memory_space=pltpu.SMEM),
            pl.BlockSpec((3, D, C), lambda f: (0, 0, 0), pipeline_mode=pl.Buffered(1)),
        ],
        out_specs=pl.BlockSpec((16, 1, SENT, C), lambda f: (0, f, 0, 0)),
        out_shape=jax.ShapeDtypeStruct((16, FRAMES, SENT, C), BF16),
        scratch_shapes=[
            pltpu.VMEM((TOK, D), BF16),
            pltpu.VMEM((TOK, 3 * C), BF16),
            pltpu.VMEM((ROWS, 3 * C), BF16),
            pltpu.VMEM((ROWS, C), BF16),
        ],
        compiler_params=pltpu.CompilerParams(vmem_limit_bytes=LIMIT),
        cost_estimate=pl.CostEstimate(
            flops=2 * FRAMES * (TOK * D * 3 * C + ROWS * TOK * 3 * C + 4 * ROWS * C * C + ROWS * TOK * C),
            bytes_accessed=FRAMES * TOK * D * 4,
            transcendentals=FRAMES * ROWS * C,
        ),
        name="attend",
    )(tokens, padded, frame_decay, clip_id, weight)


def recur_kernel(
    place_ref, att_ref, x0_ref, x1_ref, x2_ref, x3_ref, mix_ref, gate_ref, value_ref, open_ref,
    residual_ref, state_ref, decay_ref, open_out_ref, last_ref,
    normed,
):
    x = place_ref[0]
    h = pl.program_id(0)
    count = FRAMES * SHARE

    @pl.when(h == 0)
    def _():
        for s, x_ref in enumerate((x0_ref, x1_ref, x2_ref, x3_ref)):
            source = lax.rem(x + (4 - s), 4)
            pieces = []
            for c in range(2):
                for q in range(2):
                    total = None
                    for k in range(4):
                        left = att_ref[4 * source + k, :, :SHARE, :].reshape(count, C)
                        term = dot(left, mix_ref[c, k, q * C : (q + 1) * C, :])
                        total = term if total is None else total + term
                    pieces.append(total)
            residual = x_ref[...].reshape(count, D).astype(F32) + jnp.concatenate(pieces, axis=1)
            residual_ref[source] = residual
            normed[source] = scaled(residual).astype(BF16)

    rows = normed[...].reshape(4 * count, D)

    def project(ref):
        return dot(rows[:, : D // 2], ref[0, 0]) + dot(rows[:, D // 2 :], ref[1, 0])

    driven = jax.nn.sigmoid(project(gate_ref)) * project(value_ref)
    opening = project(open_ref)
    open_out_ref[0] = opening * jax.nn.sigmoid(opening)
    state = jnp.zeros((SHARE, C), F32)
    first = before = None
    decay = jnp.ones((1, C), F32)
    for f in range(4 * FRAMES):
        extra = att_ref[(f // 2) * 4 + h, f % 2, SHARE:, :].astype(F32)
        retain = jnp.exp(extra[0:1] + extra[1:2] + extra[2:3])
        clip = extra[3:4]
        factor = retain * jnp.where(clip == before, 1.0, 0.0) if f else retain
        first = first if f else clip
        before = clip
        drive = jnp.sqrt(1.0 - retain * retain)
        decay = factor * decay
        state = factor * state + drive * driven[f * SHARE : (f + 1) * SHARE]
        state_ref[0, f * SHARE : (f + 1) * SHARE, :] = state
        decay_ref[0, f : f + 1, :] = decay
    last_ref[0, :SHARE, :] = state.astype(BF16)
    last_ref[0, SHARE:, :] = jnp.broadcast_to(before, (8, C)).astype(BF16)
    decay_ref[0, 8:, :] = jnp.broadcast_to(first, (8, C))


def finish_kernel(state_ref, decay_ref, open_ref, incoming_ref, residual_ref, weight_ref, out_ref, rows):
    n = pl.program_id(0)

    @pl.when(n == 0)
    def _():
        for k in range(4):
            continues = incoming_ref[k, SHARE:, :].astype(F32) == decay_ref[k, 8:, :]
            incoming = incoming_ref[k, :SHARE, :].astype(F32) * jnp.where(continues, 1.0, 0.0)[:1]
            for f in range(4 * FRAMES):
                piece = slice(f * SHARE, (f + 1) * SHARE)
                state = state_ref[k, piece, :] + decay_ref[k, f : f + 1, :] * incoming
                rows[k, piece, :] = (state * open_ref[k, piece, :]).astype(BF16)

    total = residual_ref[...].reshape(8 * SHARE, C)
    for k in range(4):
        total = total + dot(rows[k], weight_ref[0, k])
    out_ref[...] = total.reshape(4, 1, FRAMES, SHARE, C).astype(BF16)


def place_kernel(in_ref, out_ref, held, sems, out_sems):
    copies = []
    for x in range(4):
        for k in range(4):
            size = STRIDE if k < 3 else SHARE
            i = len(copies)
            through = held.at[i, :, :size, :]
            inward = pltpu.make_async_copy(in_ref.at[x, k, :, :size, :], through, sems.at[i])
            target = out_ref.at[:, x, k * STRIDE : k * STRIDE + size, :]
            copies.append((inward, pltpu.make_async_copy(through, target, out_sems.at[i])))
            inward.start()
    for inward, outward in copies:
        inward.wait()
        outward.start()
    for inward, outward in copies:
        outward.wait()


def per_device(tokens, window_order, clip_id, attend_weight, attend_out, recur_weight, frame_decay, recur_out):
    c, z, x, h = (lax.axis_index(name) for name in ("clip", "z", "x", "head"))

    here = pl.BlockSpec(memory_space=pl.ANY)
    packed, *blocks = pl.pallas_call(
        pack_kernel,
        in_specs=[pl.BlockSpec(memory_space=pltpu.SMEM), here, here, here, here],
        out_specs=[here] * 5,
        out_shape=[jax.ShapeDtypeStruct((5 * D // 2, C), BF16)]
        + [jax.ShapeDtypeStruct((FRAMES, SHARE, D), BF16)] * 4,
        scratch_shapes=[
            pltpu.VMEM((5 * D // 2, C), BF16),
            pltpu.VMEM((4, FRAMES, SHARE, D), BF16),
            pltpu.SemaphoreType.DMA((11,)),
            pltpu.SemaphoreType.DMA((11,)),
        ],
        name="pack",
    )(jnp.stack([c, x, h]), tokens.reshape(FRAMES, 4, QUARTER, D), attend_out, recur_weight, recur_out)
    weights = lax.all_gather(packed, ("clip", "head"), axis=0).reshape(2, 4, 5 * D // 2, C)
    moved = [
        lax.ppermute(blocks[s], "x", [(i, (i + s) % 4) for i in range(4)]) if s else blocks[0] for s in range(4)
    ]

    mixed = attend(tokens, window_order, frame_decay, clip_id, attend_weight)
    mixed, *moved = lax.optimization_barrier((mixed, *moved))
    mixed = lax.all_to_all(mixed, ("x", "head"), 0, 0)

    whole = lambda shape: pl.BlockSpec(shape, lambda n: (0,) * len(shape), pipeline_mode=pl.Buffered(1))
    span = D // 2
    wide = 8 * SHARE
    residual, state, decay, opened, last = pl.pallas_call(
        recur_kernel,
        grid=(4,),
        in_specs=[
            pl.BlockSpec(memory_space=pltpu.SMEM),
            whole((16, FRAMES, SENT, C)),
            whole((FRAMES, SHARE, D)),
            whole((FRAMES, SHARE, D)),
            whole((FRAMES, SHARE, D)),
            whole((FRAMES, SHARE, D)),
            pl.BlockSpec((2, 4, span, C), lambda n: (0, 0, 0, 0)),
            pl.BlockSpec((2, 1, span, C), lambda n: (0, n, 1, 0)),
            pl.BlockSpec((2, 1, span, C), lambda n: (0, n, 2, 0)),
            pl.BlockSpec((2, 1, span, C), lambda n: (0, n, 3, 0)),
        ],
        out_specs=[
            pl.BlockSpec((4, FRAMES * SHARE, D), lambda n: (0, 0, 0)),
            pl.BlockSpec((1, wide, C), lambda n: (n, 0, 0)),
            pl.BlockSpec((1, 16, C), lambda n: (n, 0, 0)),
            pl.BlockSpec((1, wide, C), lambda n: (n, 0, 0)),
            pl.BlockSpec((1, SENT, C), lambda n: (n, 0, 0)),
        ],
        out_shape=[
            jax.ShapeDtypeStruct((4, FRAMES * SHARE, D), F32),
            jax.ShapeDtypeStruct((4, wide, C), F32),
            jax.ShapeDtypeStruct((4, 16, C), F32),
            jax.ShapeDtypeStruct((4, wide, C), F32),
            jax.ShapeDtypeStruct((4, SENT, C), BF16),
        ],
        scratch_shapes=[pltpu.VMEM((4, FRAMES * SHARE, D), BF16)],
        compiler_params=pltpu.CompilerParams(vmem_limit_bytes=LIMIT),
        name="recur",
    )(x[None], mixed, *moved, weights, weights, weights, weights)

    incoming = lax.ppermute(last, "z", [(i, i + 1) for i in range(3)])

    result = pl.pallas_call(
        finish_kernel,
        grid=(4,),
        in_specs=[
            whole((4, wide, C)),
            whole((4, 16, C)),
            whole((4, wide, C)),
            whole((4, SENT, C)),
            pl.BlockSpec((4, FRAMES * SHARE, C), lambda n: (0, 0, n)),
            pl.BlockSpec((1, 4, C, C), lambda n: (n // 2, 0, 8 + n % 2, 0)),
        ],
        out_specs=pl.BlockSpec((4, 1, FRAMES, SHARE, C), lambda n: (0, n, 0, 0, 0)),
        out_shape=jax.ShapeDtypeStruct((4, 4, FRAMES, SHARE, C), BF16),
        scratch_shapes=[pltpu.VMEM((4, wide, C), BF16)],
        compiler_params=pltpu.CompilerParams(vmem_limit_bytes=LIMIT),
        name="finish",
    )(state, decay, opened, incoming, residual, weights)

    result = lax.all_to_all(result.reshape(16, FRAMES, SHARE, C), ("x", "head"), 0, 0)
    placed = pl.pallas_call(
        place_kernel,
        in_specs=[here],
        out_specs=here,
        out_shape=jax.ShapeDtypeStruct((FRAMES, 4, QUARTER, C), BF16),
        scratch_shapes=[
            pltpu.VMEM((16, FRAMES, SHARE, C), BF16),
            pltpu.SemaphoreType.DMA((16,)),
            pltpu.SemaphoreType.DMA((16,)),
        ],
        name="place",
    )(result.reshape(4, 4, FRAMES, SHARE, C))
    return placed.reshape(FRAMES, TOK, C)


def solution(mesh):
    split = Mesh(mesh.devices.reshape(2, 4, 4, 4), ("clip", "z", "x", "head"))
    frames = ("clip", "z", "x")
    return jax.shard_map(
        per_device,
        mesh=split,
        in_specs=(
            P(frames, None, None),
            P(frames, None),
            P(frames),
            P(None, None, "head"),
            P("head", None),
            P(None, None, "head"),
            P(frames, "head"),
            P("head", None),
        ),
        out_specs=P(frames, None, "head"),
        check_vma=False,
    )
```

```python
import functools
import jax
import jax.numpy as jnp
from jax import lax
from jax.experimental import pallas as pl
from jax.experimental.pallas import tpu as pltpu
from jax.sharding import Mesh, PartitionSpec as P

HEAD = 64
WINDOW = 49
SLOT = 64
TOK = 1568
WINDOWS = TOK // WINDOW
ROWS = WINDOWS * SLOT
D = 1024
C = 256
FRAMES = 2
QUARTER = TOK // 4
STRIDE = 96
SHARE = 104
SENT = SHARE + 8
EPSILON = 1e-06
F32 = jnp.float32
BF16 = jnp.bfloat16
LIMIT = 40 * 1024 * 1024
WHOLE = 62 * 1024 * 1024


def dot(left, right):
    return jnp.dot(left, right, preferred_element_type=F32)


def dot_t(left, right):
    return lax.dot_general(left, right, (((1,), (1,)), ((), ())), preferred_element_type=F32)


def scaled(values):
    return values * lax.rsqrt(jnp.mean(values * values, axis=-1, keepdims=True) + EPSILON)


def pack_kernel(place_ref, tokens_ref, mix_ref, recur_ref, last_ref, *rest):
    packed_refs, block_refs, (packed, blocks, sems, out_sems) = rest[:2], rest[2:6], rest[6:]
    x, c, h = place_ref[0], place_ref[1], place_ref[2]
    copies = []

    def copy(source, through, target):
        i = len(copies)
        inward = pltpu.make_async_copy(source, through, sems.at[i])
        copies.append((inward, pltpu.make_async_copy(through, target, out_sems.at[i])))
        inward.start()

    for i, packed_ref in enumerate(packed_refs):
        part = c if i == 0 else 1 - c

        def pack(source, rows):
            copy(source, packed.at[i, rows, :], packed_ref.at[rows, :])

        for q in range(2):
            columns = pl.ds(pl.multiple_of(part * (2 * C) + q * C, C), C)
            pack(mix_ref.at[:, columns], slice(q * C, (q + 1) * C))
            pack(last_ref.at[:, columns], slice((8 + q) * C, (9 + q) * C))
        for k in range(3):
            half = pl.ds(pl.multiple_of(part * (D // 2), D // 2), D // 2)
            pack(recur_ref.at[k, half, :], slice((k + 1) * D // 2, (k + 2) * D // 2))
    for s, block_ref in enumerate(block_refs):
        part = tokens_ref.at[:, lax.rem(x + s, 4), pl.ds(pl.multiple_of(h * STRIDE, 16), SHARE), :]
        copy(part, blocks.at[s], block_ref)
    for inward, outward in copies:
        inward.wait()
        outward.start()
    for inward, outward in copies:
        outward.wait()


def attend_kernel(f, x_ref, order_ref, decay_ref, clip_ref, weight_ref, *rest):
    out_ref, held, weight, normed, qkv, arranged, mixed, sems = rest[-8:]
    step = 112

    def token_copy(i):
        rows = pl.ds(pl.multiple_of(i * step, 16), step)
        return pltpu.make_async_copy(x_ref.at[f, rows, :], held.at[rows, :], sems.at[i])

    weight_copy = pltpu.make_async_copy(weight_ref, weight, sems.at[TOK // step])
    for i in range(TOK // step):
        token_copy(i).start()
    weight_copy.start()

    def norm_step(i, carry):
        rows = pl.ds(pl.multiple_of(i * step, 16), step)
        token_copy(i).wait()
        normed[rows, :] = scaled(held[rows, :].astype(F32)).astype(BF16)
        return carry

    lax.fori_loop(0, TOK // step, norm_step, 0)

    weight_copy.wait()
    half = TOK // 2
    for i in range(2):
        for k in range(3):
            rows = slice(i * half, (i + 1) * half)
            qkv[rows, k * C : (k + 1) * C] = dot(normed[rows, :], weight[k]).astype(BF16)

    lanes = lax.broadcasted_iota(jnp.int32, (128, TOK), 1)
    columns = jnp.transpose(order_ref[0])
    for i in range(ROWS // 512):
        pick = jnp.concatenate(
            [jnp.where(lanes == columns[:, j : j + 1], 1.0, 0.0).astype(BF16) for j in range(4 * i, 4 * i + 4)],
            axis=0,
        )
        arranged[i * 512 : (i + 1) * 512, :] = dot(pick, qkv[...]).astype(BF16)

    lane_head = lax.broadcasted_iota(jnp.int32, (SLOT, C), 1) // HEAD
    own = [lane_head == h for h in range(4)]
    row_index = lax.broadcasted_iota(jnp.int32, (C, C), 0)
    lane_index = lax.broadcasted_iota(jnp.int32, (C, C), 1)
    together = jnp.where(row_index // HEAD == lane_index // HEAD, 1.0, 0.0).astype(BF16)
    group = 4
    lane = lax.broadcasted_iota(jnp.int32, (group * SLOT, 128), 1)
    low = lane < SLOT
    valid = (lane % SLOT) < WINDOW
    floor = -3.0e38

    def spread(block):
        return jnp.concatenate([jnp.where(own[h], block, jnp.zeros_like(block)) for h in range(4)], axis=0)

    def window_step(i, carry):
        base = i * (group * SLOT)
        scores = []
        for w in range(group):
            rows = pl.ds(pl.multiple_of(base + w * SLOT, SLOT), SLOT)
            scores.append(dot_t(arranged[rows, 0:C], spread(arranged[rows, C : 2 * C])))
        scores = jnp.concatenate(scores, axis=0) * 0.125
        pieces = []
        for side in range(2):
            piece = jnp.where(valid, scores[:, side * 128 : (side + 1) * 128], floor)
            top_low = jnp.max(jnp.where(low, piece, floor), axis=-1, keepdims=True)
            top_high = jnp.max(jnp.where(low, floor, piece), axis=-1, keepdims=True)
            pieces.append(jnp.exp(piece - jnp.where(low, top_low, top_high)))
        weights = jnp.concatenate(pieces, axis=1).astype(BF16)
        totals = dot(weights, together)
        blended = []
        for w in range(group):
            rows = pl.ds(pl.multiple_of(base + w * SLOT, SLOT), SLOT)
            blended.append(dot(weights[w * SLOT : (w + 1) * SLOT], spread(arranged[rows, 2 * C : 3 * C])))
        blended = jnp.concatenate(blended, axis=0) / totals
        mixed[pl.ds(pl.multiple_of(base, group * SLOT), group * SLOT), :] = blended.astype(BF16)
        return carry

    lax.fori_loop(0, WINDOWS // group, window_step, 0)

    decay = decay_ref[f : f + 1, :]
    clip = clip_ref[f].astype(F32)
    high = decay.astype(BF16).astype(F32)
    middle = (decay - high).astype(BF16).astype(F32)
    index = lax.broadcasted_iota(jnp.int32, (8, C), 0)
    extra = jnp.where(
        index == 0,
        high,
        jnp.where(index == 1, middle, jnp.where(index == 2, (decay - high) - middle, clip)),
    ).astype(BF16)

    def restore_step(i, carry):
        r = lax.broadcasted_iota(jnp.int32, (4 * SHARE, 128), 0)
        late = jnp.where(r >= SHARE, 8, 0) + jnp.where(r >= 2 * SHARE, 8, 0) + jnp.where(r >= 3 * SHARE, 8, 0)
        position = r - late + i * QUARTER
        pick = jnp.concatenate(
            [jnp.where(position == order_ref[0, j : j + 1, :], 1.0, 0.0).astype(BF16) for j in range(ROWS // 128)],
            axis=1,
        )
        result = dot(pick, mixed[...])
        for h in range(4):
            out_ref[4 * i + h, 0, :SHARE, :] = result[h * SHARE : (h + 1) * SHARE].astype(BF16)
            out_ref[4 * i + h, 0, SHARE:, :] = extra
        return carry

    lax.fori_loop(0, 4, restore_step, 0)


def in_windows(window_order):
    return jnp.pad(
        window_order.reshape(FRAMES, WINDOWS, WINDOW),
        ((0, 0), (0, 0), (0, SLOT - WINDOW)),
        constant_values=-1,
    ).reshape(FRAMES, ROWS // 128, 128)


def attend(f, tokens, order, frame_decay, clip_id, weight, *held):
    fixed = lambda shape, at: pl.BlockSpec(shape, lambda n: at, pipeline_mode=pl.Buffered(1))
    return pl.pallas_call(
        functools.partial(attend_kernel, f),
        grid=(1,),
        in_specs=[
            pl.BlockSpec(memory_space=pltpu.HBM),
            fixed((1, ROWS // 128, 128), (f, 0, 0)),
            fixed((FRAMES, C), (0, 0)),
            pl.BlockSpec(memory_space=pltpu.SMEM),
            pl.BlockSpec(memory_space=pltpu.HBM),
        ]
        + [pl.BlockSpec(memory_space=pltpu.HBM)] * len(held),
        out_specs=fixed((16, 1, SENT, C), (0, f, 0, 0)),
        out_shape=jax.ShapeDtypeStruct((16, FRAMES, SENT, C), BF16),
        scratch_shapes=[
            pltpu.VMEM((TOK, D), BF16),
            pltpu.VMEM((3, D, C), BF16),
            pltpu.VMEM((TOK, D), BF16),
            pltpu.VMEM((TOK, 3 * C), BF16),
            pltpu.VMEM((ROWS, 3 * C), BF16),
            pltpu.VMEM((ROWS, C), BF16),
            pltpu.SemaphoreType.DMA((15,)),
        ],
        input_output_aliases={5: 0} if held else {},
        compiler_params=pltpu.CompilerParams(vmem_limit_bytes=WHOLE),
        cost_estimate=pl.CostEstimate(
            flops=2 * (TOK * D * 3 * C + ROWS * TOK * 3 * C + 4 * ROWS * C * C + ROWS * TOK * C),
            bytes_accessed=TOK * D * 4,
            transcendentals=ROWS * C,
        ),
        name="attend",
    )(tokens, order, frame_decay, clip_id, weight, *held)


def weight_copies(place_ref, weight_refs, held, sems, first, rows):
    c, h = place_ref[1], place_ref[2]
    near, far = lax.rem(h + 3 + 2 * c, 4), lax.rem(h + 1 + 2 * c, 4)
    places = [(c, h), (1 - c, h), (c, near), (1 - c, near), (1 - c, far), (c, far)]
    places += [(c, lax.rem(h + 2, 4)), (1 - c, lax.rem(h + 2, 4))]
    return [
        pltpu.make_async_copy(
            weight_ref.at[first : first + rows, :], held.at[half, index, first : first + rows, :], sems.at[i]
        )
        for i, (weight_ref, (half, index)) in enumerate(zip(weight_refs, places))
    ]


def recur_kernel(
    place_ref, att_ref, x0_ref, x1_ref, x2_ref, x3_ref, *rest
):
    weight_refs = rest[:8]
    residual_ref, state_ref, decay_ref, open_out_ref, last_ref, normed, held, sems = rest[8:]
    x = place_ref[0]
    h = pl.program_id(0)
    count = FRAMES * SHARE

    @pl.when(h == 0)
    def _():
        mix_copies = weight_copies(place_ref, weight_refs, held, sems.at[0], 0, D // 2)
        recur_copies = weight_copies(place_ref, weight_refs, held, sems.at[1], D // 2, 3 * D // 2)
        for one in mix_copies + recur_copies:
            one.start()
        for one in mix_copies:
            one.wait()
        for s, x_ref in enumerate((x0_ref, x1_ref, x2_ref, x3_ref)):
            source = lax.rem(x + (4 - s), 4)
            pieces = []
            for c in range(2):
                for q in range(2):
                    total = None
                    for k in range(4):
                        left = att_ref[4 * source + k, :, :SHARE, :].reshape(count, C)
                        term = dot(left, held[c, k, q * C : (q + 1) * C, :])
                        total = term if total is None else total + term
                    pieces.append(total)
            residual = x_ref[...].reshape(count, D).astype(F32) + jnp.concatenate(pieces, axis=1)
            residual_ref[source] = residual
            normed[source] = scaled(residual).astype(BF16)
        for one in recur_copies:
            one.wait()

    rows = normed[...].reshape(4 * count, D)

    def project(i):
        part = slice((i + 1) * D // 2, (i + 2) * D // 2)
        return dot(rows[:, : D // 2], held[0, h, part, :]) + dot(rows[:, D // 2 :], held[1, h, part, :])

    driven = jax.nn.sigmoid(project(0)) * project(1)
    opening = project(2)
    open_out_ref[0] = opening * jax.nn.sigmoid(opening)
    state = jnp.zeros((SHARE, C), F32)
    first = before = None
    decay = jnp.ones((1, C), F32)
    for f in range(4 * FRAMES):
        extra = att_ref[(f // 2) * 4 + h, f % 2, SHARE:, :].astype(F32)
        retain = jnp.exp(extra[0:1] + extra[1:2] + extra[2:3])
        clip = extra[3:4]
        factor = retain * jnp.where(clip == before, 1.0, 0.0) if f else retain
        first = first if f else clip
        before = clip
        drive = jnp.sqrt(1.0 - retain * retain)
        decay = factor * decay
        state = factor * state + drive * driven[f * SHARE : (f + 1) * SHARE]
        state_ref[0, f * SHARE : (f + 1) * SHARE, :] = state
        decay_ref[0, f : f + 1, :] = decay
    last_ref[0, :SHARE, :] = state.astype(BF16)
    last_ref[0, SHARE:, :] = jnp.broadcast_to(before, (8, C)).astype(BF16)
    decay_ref[0, 8:, :] = jnp.broadcast_to(first, (8, C))


def finish_kernel(place_ref, state_ref, decay_ref, open_ref, incoming_ref, residual_ref, *rest):
    weight_refs = rest[:8]
    out_ref, rows, held, sems = rest[8:]
    n = pl.program_id(0)

    @pl.when(n == 0)
    def _():
        copies = weight_copies(place_ref, weight_refs, held, sems, 2 * D, D // 2)
        for one in copies:
            one.start()
        for k in range(4):
            continues = incoming_ref[k, SHARE:, :].astype(F32) == decay_ref[k, 8:, :]
            incoming = incoming_ref[k, :SHARE, :].astype(F32) * jnp.where(continues, 1.0, 0.0)[:1]
            for f in range(4 * FRAMES):
                piece = slice(f * SHARE, (f + 1) * SHARE)
                state = state_ref[k, piece, :] + decay_ref[k, f : f + 1, :] * incoming
                rows[k, piece, :] = (state * open_ref[k, piece, :]).astype(BF16)
        for one in copies:
            one.wait()

    total = residual_ref[...].reshape(8 * SHARE, C)
    part = pl.ds(pl.multiple_of(2 * D + lax.rem(n, 2) * C, C), C)
    for k in range(4):
        total = total + dot(rows[k], held[n // 2, k, part, :])
    out_ref[...] = total.reshape(4, 1, FRAMES, SHARE, C).astype(BF16)


def place_kernel(in_ref, out_ref, held, sems, out_sems):
    copies = []
    for x in range(4):
        for k in range(4):
            size = STRIDE if k < 3 else SHARE
            i = len(copies)
            through = held.at[i, :, :size, :]
            inward = pltpu.make_async_copy(in_ref.at[x, k, :, :size, :], through, sems.at[i])
            target = out_ref.at[:, x, k * STRIDE : k * STRIDE + size, :]
            copies.append((inward, pltpu.make_async_copy(through, target, out_sems.at[i])))
            inward.start()
    for inward, outward in copies:
        inward.wait()
        outward.start()
    for inward, outward in copies:
        outward.wait()


def per_device(tokens, window_order, clip_id, attend_weight, attend_out, recur_weight, frame_decay, recur_out):
    c, z, x, h = (lax.axis_index(name) for name in ("clip", "z", "x", "head"))

    place = jnp.stack([x, c, h])
    here = pl.BlockSpec(memory_space=pltpu.HBM)
    first, second, *blocks = pl.pallas_call(
        pack_kernel,
        in_specs=[pl.BlockSpec(memory_space=pltpu.SMEM), here, here, here, here],
        out_specs=[here] * 6,
        out_shape=[jax.ShapeDtypeStruct((5 * D // 2, C), BF16)] * 2
        + [jax.ShapeDtypeStruct((FRAMES, SHARE, D), BF16)] * 4,
        scratch_shapes=[
            pltpu.VMEM((2, 5 * D // 2, C), BF16),
            pltpu.VMEM((4, FRAMES, SHARE, D), BF16),
            pltpu.SemaphoreType.DMA((18,)),
            pltpu.SemaphoreType.DMA((18,)),
        ],
        name="pack",
    )(place, tokens.reshape(FRAMES, 4, QUARTER, D), attend_out, recur_weight, recur_out)
    def pinned(value):
        return pltpu.with_memory_space_constraint(value, pltpu.HBM)

    def onward(value):
        pairs = [(i, (i + 1) % 4) for i in range(4)] + [(4 + i, 4 + (i + 3) % 4) for i in range(4)]
        return lax.ppermute(value, ("clip", "head"), pairs)

    def across(value):
        return lax.ppermute(value, "clip", [(0, 1), (1, 0)])

    near_first = onward(first)
    near_second = onward(second)
    moved = [
        lax.ppermute(blocks[s], "x", [(i, (i + s) % 4) for i in range(4)]) if s else blocks[0] for s in range(4)
    ]

    order = in_windows(window_order)
    tokens, attend_weight = pinned(tokens), pinned(attend_weight)
    mixed = attend(0, tokens, order, frame_decay, clip_id, attend_weight)
    mixed, near_first = lax.optimization_barrier((mixed, near_first))
    far_first = onward(near_first)
    other_first = across(near_first)
    mixed = attend(1, tokens, order, frame_decay, clip_id, attend_weight, mixed)
    mixed, near_second, far_first, other_first, *moved = lax.optimization_barrier(
        (mixed, near_second, far_first, other_first, *moved)
    )
    other_second = across(near_second)
    far_second = across(far_first)
    weights = (first, second, near_first, near_second, other_first, other_second, far_first, far_second)
    mixed = lax.all_to_all(mixed, ("x", "head"), 0, 0)

    whole = lambda shape: pl.BlockSpec(shape, lambda n: (0,) * len(shape), pipeline_mode=pl.Buffered(1))
    wide = 8 * SHARE
    residual, state, decay, opened, last = pl.pallas_call(
        recur_kernel,
        grid=(4,),
        in_specs=[
            pl.BlockSpec(memory_space=pltpu.SMEM),
            whole((16, FRAMES, SENT, C)),
            whole((FRAMES, SHARE, D)),
            whole((FRAMES, SHARE, D)),
            whole((FRAMES, SHARE, D)),
            whole((FRAMES, SHARE, D)),
            *[here] * 8,
        ],
        out_specs=[
            pl.BlockSpec((4, FRAMES * SHARE, D), lambda n: (0, 0, 0)),
            pl.BlockSpec((1, wide, C), lambda n: (n, 0, 0)),
            pl.BlockSpec((1, 16, C), lambda n: (n, 0, 0)),
            pl.BlockSpec((1, wide, C), lambda n: (n, 0, 0)),
            pl.BlockSpec((1, SENT, C), lambda n: (n, 0, 0)),
        ],
        out_shape=[
            jax.ShapeDtypeStruct((4, FRAMES * SHARE, D), F32),
            jax.ShapeDtypeStruct((4, wide, C), F32),
            jax.ShapeDtypeStruct((4, 16, C), F32),
            jax.ShapeDtypeStruct((4, wide, C), F32),
            jax.ShapeDtypeStruct((4, SENT, C), BF16),
        ],
        scratch_shapes=[
            pltpu.VMEM((4, FRAMES * SHARE, D), BF16),
            pltpu.VMEM((2, 4, 2 * D, C), BF16),
            pltpu.SemaphoreType.DMA((2, 8)),
        ],
        compiler_params=pltpu.CompilerParams(vmem_limit_bytes=LIMIT),
        name="recur",
    )(place, mixed, *map(pinned, moved), *map(pinned, weights))

    incoming = lax.ppermute(last, "z", [(i, i + 1) for i in range(3)])

    result = pl.pallas_call(
        finish_kernel,
        grid=(4,),
        in_specs=[
            pl.BlockSpec(memory_space=pltpu.SMEM),
            whole((4, wide, C)),
            whole((4, 16, C)),
            whole((4, wide, C)),
            whole((4, SENT, C)),
            pl.BlockSpec((4, FRAMES * SHARE, C), lambda n: (0, 0, n)),
            *[here] * 8,
        ],
        out_specs=pl.BlockSpec((4, 1, FRAMES, SHARE, C), lambda n: (0, n, 0, 0, 0)),
        out_shape=jax.ShapeDtypeStruct((4, 4, FRAMES, SHARE, C), BF16),
        scratch_shapes=[
            pltpu.VMEM((4, wide, C), BF16),
            pltpu.VMEM((2, 4, 5 * D // 2, C), BF16),
            pltpu.SemaphoreType.DMA((8,)),
        ],
        compiler_params=pltpu.CompilerParams(vmem_limit_bytes=LIMIT),
        name="finish",
    )(place, state, decay, opened, incoming, residual, *map(pinned, weights))

    result = lax.all_to_all(result.reshape(16, FRAMES, SHARE, C), ("x", "head"), 0, 0)
    placed = pl.pallas_call(
        place_kernel,
        in_specs=[here],
        out_specs=here,
        out_shape=jax.ShapeDtypeStruct((FRAMES, 4, QUARTER, C), BF16),
        scratch_shapes=[
            pltpu.VMEM((16, FRAMES, SHARE, C), BF16),
            pltpu.SemaphoreType.DMA((16,)),
            pltpu.SemaphoreType.DMA((16,)),
        ],
        name="place",
    )(result.reshape(4, 4, FRAMES, SHARE, C))
    return placed.reshape(FRAMES, TOK, C)


def solution(mesh):
    split = Mesh(mesh.devices.reshape(2, 4, 4, 4), ("clip", "z", "x", "head"))
    frames = ("clip", "z", "x")
    return jax.shard_map(
        per_device,
        mesh=split,
        in_specs=(
            P(frames, None, None),
            P(frames, None),
            P(frames),
            P(None, None, "head"),
            P("head", None),
            P(None, None, "head"),
            P(frames, "head"),
            P("head", None),
        ),
        out_specs=P(frames, None, "head"),
        check_vma=False,
    )
```

```python
import functools
import jax
import jax.numpy as jnp
from jax import lax
from jax.experimental import pallas as pl
from jax.experimental.pallas import tpu as pltpu
from jax.sharding import Mesh, PartitionSpec as P

HEAD = 64
WINDOW = 49
SLOT = 64
TOK = 1568
WINDOWS = TOK // WINDOW
ROWS = WINDOWS * SLOT
D = 1024
C = 256
FRAMES = 2
QUARTER = TOK // 4
STRIDE = 96
SHARE = 104
SENT = SHARE + 8
EPSILON = 1e-06
F32 = jnp.float32
BF16 = jnp.bfloat16
LIMIT = 40 * 1024 * 1024
WHOLE = 62 * 1024 * 1024


def dot(left, right):
    return jnp.dot(left, right, preferred_element_type=F32)


def dot_t(left, right):
    return lax.dot_general(left, right, (((1,), (1,)), ((), ())), preferred_element_type=F32)


def scaled(values):
    return values * lax.rsqrt(jnp.mean(values * values, axis=-1, keepdims=True) + EPSILON)


def pack_kernel(place_ref, tokens_ref, mix_ref, recur_ref, last_ref, *rest):
    packed_refs, block_refs, (packed, blocks, sems, out_sems) = rest[:2], rest[2:6], rest[6:]
    x, c, h = place_ref[0], place_ref[1], place_ref[2]
    copies = []

    def copy(source, through, target):
        i = len(copies)
        inward = pltpu.make_async_copy(source, through, sems.at[i])
        copies.append((inward, pltpu.make_async_copy(through, target, out_sems.at[i])))
        inward.start()

    for i, packed_ref in enumerate(packed_refs):
        part = c if i == 0 else 1 - c

        def pack(source, rows):
            copy(source, packed.at[i, rows, :], packed_ref.at[rows, :])

        for q in range(2):
            columns = pl.ds(pl.multiple_of(part * (2 * C) + q * C, C), C)
            pack(mix_ref.at[:, columns], slice(q * C, (q + 1) * C))
            pack(last_ref.at[:, columns], slice((8 + q) * C, (9 + q) * C))
        for k in range(3):
            half = pl.ds(pl.multiple_of(part * (D // 2), D // 2), D // 2)
            pack(recur_ref.at[k, half, :], slice((k + 1) * D // 2, (k + 2) * D // 2))
    for s, block_ref in enumerate(block_refs):
        part = tokens_ref.at[:, lax.rem(x + s, 4), pl.ds(pl.multiple_of(h * STRIDE, 16), SHARE), :]
        copy(part, blocks.at[s], block_ref)
    for inward, outward in copies:
        inward.wait()
        outward.start()
    for inward, outward in copies:
        outward.wait()


def attend_kernel(f, x_ref, order_ref, decay_ref, clip_ref, weight_ref, *rest):
    out_ref, held, weight, normed, qkv, arranged, mixed, sems = rest[-8:]
    step = 224

    def token_copy(i):
        rows = pl.ds(pl.multiple_of(i * step, 16), step)
        return pltpu.make_async_copy(x_ref.at[f, rows, :], held.at[rows, :], sems.at[i])

    weight_copy = pltpu.make_async_copy(weight_ref, weight, sems.at[TOK // step])
    for i in range(TOK // step):
        token_copy(i).start()
    weight_copy.start()

    def norm_step(i, carry):
        rows = pl.ds(pl.multiple_of(i * step, 16), step)
        token_copy(i).wait()
        normed[rows, :] = scaled(held[rows, :].astype(F32)).astype(BF16)
        return carry

    lax.fori_loop(0, TOK // step, norm_step, 0)

    weight_copy.wait()
    half = TOK // 2
    for i in range(2):
        for k in range(3):
            rows = slice(i * half, (i + 1) * half)
            qkv[rows, k * C : (k + 1) * C] = dot(normed[rows, :], weight[k]).astype(BF16)

    lanes = lax.broadcasted_iota(jnp.int32, (128, TOK), 1)
    columns = jnp.transpose(order_ref[0])
    for i in range(ROWS // 512):
        pick = jnp.concatenate(
            [jnp.where(lanes == columns[:, j : j + 1], 1.0, 0.0).astype(BF16) for j in range(4 * i, 4 * i + 4)],
            axis=0,
        )
        arranged[i * 512 : (i + 1) * 512, :] = dot(pick, qkv[...]).astype(BF16)

    lane_head = lax.broadcasted_iota(jnp.int32, (SLOT, C), 1) // HEAD
    own = [lane_head == h for h in range(4)]
    row_index = lax.broadcasted_iota(jnp.int32, (C, C), 0)
    lane_index = lax.broadcasted_iota(jnp.int32, (C, C), 1)
    together = jnp.where(row_index // HEAD == lane_index // HEAD, 1.0, 0.0).astype(BF16)
    group = 16
    lane = lax.broadcasted_iota(jnp.int32, (group * SLOT, 128), 1)
    low = lane < SLOT
    valid = (lane % SLOT) < WINDOW
    floor = -3.0e38

    def spread(block):
        return jnp.concatenate([jnp.where(own[h], block, jnp.zeros_like(block)) for h in range(4)], axis=0)

    def window_step(i, carry):
        base = i * (group * SLOT)
        scores = []
        for w in range(group):
            rows = pl.ds(pl.multiple_of(base + w * SLOT, SLOT), SLOT)
            scores.append(dot_t(arranged[rows, 0:C], spread(arranged[rows, C : 2 * C])))
        scores = jnp.concatenate(scores, axis=0) * 0.125
        pieces = []
        for side in range(2):
            piece = jnp.where(valid, scores[:, side * 128 : (side + 1) * 128], floor)
            top_low = jnp.max(jnp.where(low, piece, floor), axis=-1, keepdims=True)
            top_high = jnp.max(jnp.where(low, floor, piece), axis=-1, keepdims=True)
            pieces.append(jnp.exp(piece - jnp.where(low, top_low, top_high)))
        weights = jnp.concatenate(pieces, axis=1).astype(BF16)
        totals = dot(weights, together)
        blended = []
        for w in range(group):
            rows = pl.ds(pl.multiple_of(base + w * SLOT, SLOT), SLOT)
            blended.append(dot(weights[w * SLOT : (w + 1) * SLOT], spread(arranged[rows, 2 * C : 3 * C])))
        blended = jnp.concatenate(blended, axis=0) / totals
        mixed[pl.ds(pl.multiple_of(base, group * SLOT), group * SLOT), :] = blended.astype(BF16)
        return carry

    lax.fori_loop(0, WINDOWS // group, window_step, 0)

    decay = decay_ref[f : f + 1, :]
    clip = clip_ref[f].astype(F32)
    high = decay.astype(BF16).astype(F32)
    middle = (decay - high).astype(BF16).astype(F32)
    index = lax.broadcasted_iota(jnp.int32, (8, C), 0)
    extra = jnp.where(
        index == 0,
        high,
        jnp.where(index == 1, middle, jnp.where(index == 2, (decay - high) - middle, clip)),
    ).astype(BF16)

    def restore_step(i, carry):
        r = lax.broadcasted_iota(jnp.int32, (4 * SHARE, 128), 0)
        late = jnp.where(r >= SHARE, 8, 0) + jnp.where(r >= 2 * SHARE, 8, 0) + jnp.where(r >= 3 * SHARE, 8, 0)
        position = r - late + i * QUARTER
        pick = jnp.concatenate(
            [jnp.where(position == order_ref[0, j : j + 1, :], 1.0, 0.0).astype(BF16) for j in range(ROWS // 128)],
            axis=1,
        )
        result = dot(pick, mixed[...])
        for h in range(4):
            out_ref[4 * i + h, 0, :SHARE, :] = result[h * SHARE : (h + 1) * SHARE].astype(BF16)
            out_ref[4 * i + h, 0, SHARE:, :] = extra
        return carry

    lax.fori_loop(0, 4, restore_step, 0, unroll=4)


def in_windows(window_order):
    return jnp.pad(
        window_order.reshape(FRAMES, WINDOWS, WINDOW),
        ((0, 0), (0, 0), (0, SLOT - WINDOW)),
        constant_values=-1,
    ).reshape(FRAMES, ROWS // 128, 128)


def attend(f, tokens, order, frame_decay, clip_id, weight, *held):
    fixed = lambda shape, at: pl.BlockSpec(shape, lambda n: at, pipeline_mode=pl.Buffered(1))
    return pl.pallas_call(
        functools.partial(attend_kernel, f),
        grid=(1,),
        in_specs=[
            pl.BlockSpec(memory_space=pltpu.HBM),
            fixed((1, ROWS // 128, 128), (f, 0, 0)),
            fixed((FRAMES, C), (0, 0)),
            pl.BlockSpec(memory_space=pltpu.SMEM),
            pl.BlockSpec(memory_space=pltpu.HBM),
        ]
        + [pl.BlockSpec(memory_space=pltpu.HBM)] * len(held),
        out_specs=fixed((16, 1, SENT, C), (0, f, 0, 0)),
        out_shape=jax.ShapeDtypeStruct((16, FRAMES, SENT, C), BF16),
        scratch_shapes=[
            pltpu.VMEM((TOK, D), BF16),
            pltpu.VMEM((3, D, C), BF16),
            pltpu.VMEM((TOK, D), BF16),
            pltpu.VMEM((TOK, 3 * C), BF16),
            pltpu.VMEM((ROWS, 3 * C), BF16),
            pltpu.VMEM((ROWS, C), BF16),
            pltpu.SemaphoreType.DMA((15,)),
        ],
        input_output_aliases={5: 0} if held else {},
        compiler_params=pltpu.CompilerParams(vmem_limit_bytes=WHOLE),
        cost_estimate=pl.CostEstimate(
            flops=2 * (TOK * D * 3 * C + ROWS * TOK * 3 * C + 4 * ROWS * C * C + ROWS * TOK * C),
            bytes_accessed=TOK * D * 4,
            transcendentals=ROWS * C,
        ),
        name="attend",
    )(tokens, order, frame_decay, clip_id, weight, *held)


def weight_copies(place_ref, weight_refs, held, sems, first, rows):
    c, h = place_ref[1], place_ref[2]
    near, far = lax.rem(h + 3 + 2 * c, 4), lax.rem(h + 1 + 2 * c, 4)
    places = [(c, h), (1 - c, h), (c, near), (1 - c, near), (1 - c, far), (c, far)]
    places += [(c, lax.rem(h + 2, 4)), (1 - c, lax.rem(h + 2, 4))]
    return [
        pltpu.make_async_copy(
            weight_ref.at[first : first + rows, :], held.at[half, index, first : first + rows, :], sems.at[i]
        )
        for i, (weight_ref, (half, index)) in enumerate(zip(weight_refs, places))
    ]


def recur_kernel(
    place_ref, att_ref, x0_ref, x1_ref, x2_ref, x3_ref, *rest
):
    weight_refs = rest[:8]
    residual_ref, state_ref, decay_ref, open_out_ref, last_ref, normed, held, sems = rest[8:]
    x = place_ref[0]
    h = pl.program_id(0)
    count = FRAMES * SHARE

    @pl.when(h == 0)
    def _():
        mix_copies = weight_copies(place_ref, weight_refs, held, sems.at[0], 0, D // 2)
        recur_copies = weight_copies(place_ref, weight_refs, held, sems.at[1], D // 2, 3 * D // 2)
        for one in mix_copies + recur_copies:
            one.start()
        for one in mix_copies:
            one.wait()
        for s, x_ref in enumerate((x0_ref, x1_ref, x2_ref, x3_ref)):
            source = lax.rem(x + (4 - s), 4)
            pieces = []
            for c in range(2):
                for q in range(2):
                    total = None
                    for k in range(4):
                        left = att_ref[4 * source + k, :, :SHARE, :].reshape(count, C)
                        term = dot(left, held[c, k, q * C : (q + 1) * C, :])
                        total = term if total is None else total + term
                    pieces.append(total)
            residual = x_ref[...].reshape(count, D).astype(F32) + jnp.concatenate(pieces, axis=1)
            residual_ref[source] = residual
            normed[source] = scaled(residual).astype(BF16)
        for one in recur_copies:
            one.wait()

    rows = normed[...].reshape(4 * count, D)

    def project(i):
        part = slice((i + 1) * D // 2, (i + 2) * D // 2)
        return dot(rows[:, : D // 2], held[0, h, part, :]) + dot(rows[:, D // 2 :], held[1, h, part, :])

    driven = jax.nn.sigmoid(project(0)) * project(1)
    opening = project(2)
    open_out_ref[0] = opening * jax.nn.sigmoid(opening)
    state = jnp.zeros((SHARE, C), F32)
    first = before = None
    decay = jnp.ones((1, C), F32)
    for f in range(4 * FRAMES):
        extra = att_ref[(f // 2) * 4 + h, f % 2, SHARE:, :].astype(F32)
        retain = jnp.exp(extra[0:1] + extra[1:2] + extra[2:3])
        clip = extra[3:4]
        factor = retain * jnp.where(clip == before, 1.0, 0.0) if f else retain
        first = first if f else clip
        before = clip
        drive = jnp.sqrt(1.0 - retain * retain)
        decay = factor * decay
        state = factor * state + drive * driven[f * SHARE : (f + 1) * SHARE]
        state_ref[0, f * SHARE : (f + 1) * SHARE, :] = state
        decay_ref[0, f : f + 1, :] = decay
    last_ref[0, :SHARE, :] = state.astype(BF16)
    last_ref[0, SHARE:, :] = jnp.broadcast_to(before, (8, C)).astype(BF16)
    decay_ref[0, 8:, :] = jnp.broadcast_to(first, (8, C))


def finish_kernel(place_ref, state_ref, decay_ref, open_ref, incoming_ref, residual_ref, *rest):
    weight_refs = rest[:8]
    out_ref, rows, held, sems = rest[8:]
    n = pl.program_id(0)

    @pl.when(n == 0)
    def _():
        copies = weight_copies(place_ref, weight_refs, held, sems, 2 * D, D // 2)
        for one in copies:
            one.start()
        for k in range(4):
            continues = incoming_ref[k, SHARE:, :].astype(F32) == decay_ref[k, 8:, :]
            incoming = incoming_ref[k, :SHARE, :].astype(F32) * jnp.where(continues, 1.0, 0.0)[:1]
            for f in range(4 * FRAMES):
                piece = slice(f * SHARE, (f + 1) * SHARE)
                state = state_ref[k, piece, :] + decay_ref[k, f : f + 1, :] * incoming
                rows[k, piece, :] = (state * open_ref[k, piece, :]).astype(BF16)
        for one in copies:
            one.wait()

    total = residual_ref[...].reshape(8 * SHARE, C)
    part = pl.ds(pl.multiple_of(2 * D + lax.rem(n, 2) * C, C), C)
    for k in range(4):
        total = total + dot(rows[k], held[n // 2, k, part, :])
    out_ref[...] = total.reshape(4, 1, FRAMES, SHARE, C).astype(BF16)


def place_kernel(in_ref, out_ref, held, sems, out_sems):
    copies = []
    for x in range(4):
        for k in range(4):
            size = STRIDE if k < 3 else SHARE
            i = len(copies)
            through = held.at[i, :, :size, :]
            inward = pltpu.make_async_copy(in_ref.at[x, k, :, :size, :], through, sems.at[i])
            target = out_ref.at[:, x, k * STRIDE : k * STRIDE + size, :]
            copies.append((inward, pltpu.make_async_copy(through, target, out_sems.at[i])))
            inward.start()
    for inward, outward in copies:
        inward.wait()
        outward.start()
    for inward, outward in copies:
        outward.wait()


def per_device(tokens, window_order, clip_id, attend_weight, attend_out, recur_weight, frame_decay, recur_out):
    c, z, x, h = (lax.axis_index(name) for name in ("clip", "z", "x", "head"))

    place = jnp.stack([x, c, h])
    here = pl.BlockSpec(memory_space=pltpu.HBM)
    first, second, *blocks = pl.pallas_call(
        pack_kernel,
        in_specs=[pl.BlockSpec(memory_space=pltpu.SMEM), here, here, here, here],
        out_specs=[here] * 6,
        out_shape=[jax.ShapeDtypeStruct((5 * D // 2, C), BF16)] * 2
        + [jax.ShapeDtypeStruct((FRAMES, SHARE, D), BF16)] * 4,
        scratch_shapes=[
            pltpu.VMEM((2, 5 * D // 2, C), BF16),
            pltpu.VMEM((4, FRAMES, SHARE, D), BF16),
            pltpu.SemaphoreType.DMA((18,)),
            pltpu.SemaphoreType.DMA((18,)),
        ],
        name="pack",
    )(place, tokens.reshape(FRAMES, 4, QUARTER, D), attend_out, recur_weight, recur_out)
    def pinned(value):
        return pltpu.with_memory_space_constraint(value, pltpu.HBM)

    def onward(value):
        pairs = [(i, (i + 1) % 4) for i in range(4)] + [(4 + i, 4 + (i + 3) % 4) for i in range(4)]
        return lax.ppermute(value, ("clip", "head"), pairs)

    def across(value):
        return lax.ppermute(value, "clip", [(0, 1), (1, 0)])

    near_first = onward(first)
    near_second = onward(second)
    moved = [
        lax.ppermute(blocks[s], "x", [(i, (i + s) % 4) for i in range(4)]) if s else blocks[0] for s in range(4)
    ]

    order = in_windows(window_order)
    tokens, attend_weight = pinned(tokens), pinned(attend_weight)
    mixed = attend(0, tokens, order, frame_decay, clip_id, attend_weight)
    mixed, near_first, moved[1], moved[3] = lax.optimization_barrier((mixed, near_first, moved[1], moved[3]))
    far_first = onward(near_first)
    other_first = across(near_first)
    mixed = attend(1, tokens, order, frame_decay, clip_id, attend_weight, mixed)
    mixed, near_second, other_first, *moved = lax.optimization_barrier((mixed, near_second, other_first, *moved))
    other_second = across(near_second)
    far_second = across(far_first)
    weights = (first, second, near_first, near_second, other_first, other_second, far_first, far_second)
    mixed = lax.all_to_all(mixed, ("x", "head"), 0, 0)

    whole = lambda shape: pl.BlockSpec(shape, lambda n: (0,) * len(shape), pipeline_mode=pl.Buffered(1))
    wide = 8 * SHARE
    residual, state, decay, opened, last = pl.pallas_call(
        recur_kernel,
        grid=(4,),
        in_specs=[
            pl.BlockSpec(memory_space=pltpu.SMEM),
            whole((16, FRAMES, SENT, C)),
            whole((FRAMES, SHARE, D)),
            whole((FRAMES, SHARE, D)),
            whole((FRAMES, SHARE, D)),
            whole((FRAMES, SHARE, D)),
            *[here] * 8,
        ],
        out_specs=[
            pl.BlockSpec((4, FRAMES * SHARE, D), lambda n: (0, 0, 0)),
            pl.BlockSpec((1, wide, C), lambda n: (n, 0, 0)),
            pl.BlockSpec((1, 16, C), lambda n: (n, 0, 0)),
            pl.BlockSpec((1, wide, C), lambda n: (n, 0, 0)),
            pl.BlockSpec((1, SENT, C), lambda n: (n, 0, 0)),
        ],
        out_shape=[
            jax.ShapeDtypeStruct((4, FRAMES * SHARE, D), F32),
            jax.ShapeDtypeStruct((4, wide, C), F32),
            jax.ShapeDtypeStruct((4, 16, C), F32),
            jax.ShapeDtypeStruct((4, wide, C), F32),
            jax.ShapeDtypeStruct((4, SENT, C), BF16),
        ],
        scratch_shapes=[
            pltpu.VMEM((4, FRAMES * SHARE, D), BF16),
            pltpu.VMEM((2, 4, 2 * D, C), BF16),
            pltpu.SemaphoreType.DMA((2, 8)),
        ],
        compiler_params=pltpu.CompilerParams(vmem_limit_bytes=LIMIT),
        name="recur",
    )(place, mixed, *map(pinned, moved), *map(pinned, weights))

    incoming = lax.ppermute(last, "z", [(i, i + 1) for i in range(3)])

    result = pl.pallas_call(
        finish_kernel,
        grid=(4,),
        in_specs=[
            pl.BlockSpec(memory_space=pltpu.SMEM),
            whole((4, wide, C)),
            whole((4, 16, C)),
            whole((4, wide, C)),
            whole((4, SENT, C)),
            pl.BlockSpec((4, FRAMES * SHARE, C), lambda n: (0, 0, n)),
            *[here] * 8,
        ],
        out_specs=pl.BlockSpec((4, 1, FRAMES, SHARE, C), lambda n: (0, n, 0, 0, 0)),
        out_shape=jax.ShapeDtypeStruct((4, 4, FRAMES, SHARE, C), BF16),
        scratch_shapes=[
            pltpu.VMEM((4, wide, C), BF16),
            pltpu.VMEM((2, 4, 5 * D // 2, C), BF16),
            pltpu.SemaphoreType.DMA((8,)),
        ],
        compiler_params=pltpu.CompilerParams(vmem_limit_bytes=LIMIT),
        name="finish",
    )(place, state, decay, opened, incoming, residual, *map(pinned, weights))

    result = lax.all_to_all(result.reshape(16, FRAMES, SHARE, C), ("x", "head"), 0, 0)
    placed = pl.pallas_call(
        place_kernel,
        in_specs=[here],
        out_specs=here,
        out_shape=jax.ShapeDtypeStruct((FRAMES, 4, QUARTER, C), BF16),
        scratch_shapes=[
            pltpu.VMEM((16, FRAMES, SHARE, C), BF16),
            pltpu.SemaphoreType.DMA((16,)),
            pltpu.SemaphoreType.DMA((16,)),
        ],
        name="place",
    )(result.reshape(4, 4, FRAMES, SHARE, C))
    return placed.reshape(FRAMES, TOK, C)


def solution(mesh):
    split = Mesh(mesh.devices.reshape(2, 4, 4, 4), ("clip", "z", "x", "head"))
    frames = ("clip", "z", "x")
    return jax.shard_map(
        per_device,
        mesh=split,
        in_specs=(
            P(frames, None, None),
            P(frames, None),
            P(frames),
            P(None, None, "head"),
            P("head", None),
            P(None, None, "head"),
            P(frames, "head"),
            P("head", None),
        ),
        out_specs=P(frames, None, "head"),
        check_vma=False,
    )
```

```python
import functools
import jax
import jax.numpy as jnp
from jax import lax
from jax.experimental import pallas as pl
from jax.experimental.pallas import tpu as pltpu
from jax.sharding import Mesh, PartitionSpec as P

HEAD = 64
WINDOW = 49
SLOT = 64
TOK = 1568
WINDOWS = TOK // WINDOW
ROWS = WINDOWS * SLOT
D = 1024
C = 256
FRAMES = 2
QUARTER = TOK // 4
STRIDE = 96
SHARE = 104
SENT = SHARE + 8
EPSILON = 1e-06
F32 = jnp.float32
BF16 = jnp.bfloat16
LIMIT = 40 * 1024 * 1024
WHOLE = 62 * 1024 * 1024


def dot(left, right):
    return jnp.dot(left, right, preferred_element_type=F32)


def dot_t(left, right):
    return lax.dot_general(left, right, (((1,), (1,)), ((), ())), preferred_element_type=F32)


def scaled(values):
    return values * lax.rsqrt(jnp.mean(values * values, axis=-1, keepdims=True) + EPSILON)


def pack_kernel(place_ref, tokens_ref, mix_ref, recur_ref, last_ref, *rest):
    packed_refs, block_refs, (packed, blocks, sems, out_sems) = rest[:2], rest[2:6], rest[6:]
    x, c, h = place_ref[0], place_ref[1], place_ref[2]
    copies = []

    def copy(source, through, target):
        i = len(copies)
        inward = pltpu.make_async_copy(source, through, sems.at[i])
        copies.append((inward, pltpu.make_async_copy(through, target, out_sems.at[i])))
        inward.start()

    for i, packed_ref in enumerate(packed_refs):
        part = c if i == 0 else 1 - c

        def pack(source, rows):
            copy(source, packed.at[i, rows, :], packed_ref.at[rows, :])

        for q in range(2):
            columns = pl.ds(pl.multiple_of(part * (2 * C) + q * C, C), C)
            pack(mix_ref.at[:, columns], slice(q * C, (q + 1) * C))
            pack(last_ref.at[:, columns], slice((8 + q) * C, (9 + q) * C))
        for k in range(3):
            half = pl.ds(pl.multiple_of(part * (D // 2), D // 2), D // 2)
            pack(recur_ref.at[k, half, :], slice((k + 1) * D // 2, (k + 2) * D // 2))
    for s, block_ref in enumerate(block_refs):
        part = tokens_ref.at[:, lax.rem(x + s, 4), pl.ds(pl.multiple_of(h * STRIDE, 16), SHARE), :]
        copy(part, blocks.at[s], block_ref)
    for inward, outward in copies:
        inward.wait()
        outward.start()
    for inward, outward in copies:
        outward.wait()


def attend_kernel(f, x_ref, order_ref, decay_ref, clip_ref, weight_ref, *rest):
    out_ref, held, weight, normed, qkv, arranged, mixed, sems = rest[-8:]
    step = 224

    def token_copy(i):
        rows = pl.ds(pl.multiple_of(i * step, 16), step)
        return pltpu.make_async_copy(x_ref.at[f, rows, :], held.at[rows, :], sems.at[i])

    weight_copy = pltpu.make_async_copy(weight_ref, weight, sems.at[TOK // step])
    for i in range(TOK // step):
        token_copy(i).start()
    weight_copy.start()

    def norm_step(i, carry):
        rows = pl.ds(pl.multiple_of(i * step, 16), step)
        token_copy(i).wait()
        normed[rows, :] = scaled(held[rows, :].astype(F32)).astype(BF16)
        return carry

    lax.fori_loop(0, TOK // step, norm_step, 0)

    weight_copy.wait()
    half = TOK // 2
    for i in range(2):
        for k in range(3):
            rows = slice(i * half, (i + 1) * half)
            qkv[rows, k * C : (k + 1) * C] = dot(normed[rows, :], weight[k]).astype(BF16)

    lanes = lax.broadcasted_iota(jnp.int32, (128, TOK), 1)
    columns = jnp.transpose(order_ref[0])
    for i in range(ROWS // 512):
        pick = jnp.concatenate(
            [jnp.where(lanes == columns[:, j : j + 1], 1.0, 0.0).astype(BF16) for j in range(4 * i, 4 * i + 4)],
            axis=0,
        )
        arranged[i * 512 : (i + 1) * 512, :] = dot(pick, qkv[...]).astype(BF16)

    lane_head = lax.broadcasted_iota(jnp.int32, (SLOT, C), 1) // HEAD
    own = [lane_head == h for h in range(4)]
    row_index = lax.broadcasted_iota(jnp.int32, (C, C), 0)
    lane_index = lax.broadcasted_iota(jnp.int32, (C, C), 1)
    together = jnp.where(row_index // HEAD == lane_index // HEAD, 1.0, 0.0).astype(BF16)
    group = 32
    lane = lax.broadcasted_iota(jnp.int32, (group * SLOT, 128), 1)
    low = lane < SLOT
    valid = (lane % SLOT) < WINDOW
    floor = -3.0e38

    def spread(block):
        return jnp.concatenate([jnp.where(own[h], block, jnp.zeros_like(block)) for h in range(4)], axis=0)

    def window_step(i, carry):
        base = i * (group * SLOT)
        scores = []
        for w in range(group):
            rows = pl.ds(pl.multiple_of(base + w * SLOT, SLOT), SLOT)
            scores.append(dot_t(arranged[rows, 0:C], spread(arranged[rows, C : 2 * C])))
        scores = jnp.concatenate(scores, axis=0) * 0.125
        pieces = []
        for side in range(2):
            piece = jnp.where(valid, scores[:, side * 128 : (side + 1) * 128], floor)
            top_low = jnp.max(jnp.where(low, piece, floor), axis=-1, keepdims=True)
            top_high = jnp.max(jnp.where(low, floor, piece), axis=-1, keepdims=True)
            pieces.append(jnp.exp(piece - jnp.where(low, top_low, top_high)))
        weights = jnp.concatenate(pieces, axis=1).astype(BF16)
        totals = dot(weights, together)
        blended = []
        for w in range(group):
            rows = pl.ds(pl.multiple_of(base + w * SLOT, SLOT), SLOT)
            blended.append(dot(weights[w * SLOT : (w + 1) * SLOT], spread(arranged[rows, 2 * C : 3 * C])))
        blended = jnp.concatenate(blended, axis=0) / totals
        mixed[pl.ds(pl.multiple_of(base, group * SLOT), group * SLOT), :] = blended.astype(BF16)
        return carry

    lax.fori_loop(0, WINDOWS // group, window_step, 0)

    decay = decay_ref[f : f + 1, :]
    clip = clip_ref[f].astype(F32)
    high = decay.astype(BF16).astype(F32)
    middle = (decay - high).astype(BF16).astype(F32)
    index = lax.broadcasted_iota(jnp.int32, (8, C), 0)
    extra = jnp.where(
        index == 0,
        high,
        jnp.where(index == 1, middle, jnp.where(index == 2, (decay - high) - middle, clip)),
    ).astype(BF16)

    def restore_step(i, carry):
        r = lax.broadcasted_iota(jnp.int32, (4 * SHARE, 128), 0)
        late = jnp.where(r >= SHARE, 8, 0) + jnp.where(r >= 2 * SHARE, 8, 0) + jnp.where(r >= 3 * SHARE, 8, 0)
        position = r - late + i * QUARTER
        pick = jnp.concatenate(
            [jnp.where(position == order_ref[0, j : j + 1, :], 1.0, 0.0).astype(BF16) for j in range(ROWS // 128)],
            axis=1,
        )
        result = dot(pick, mixed[...])
        for h in range(4):
            out_ref[4 * i + h, 0, :SHARE, :] = result[h * SHARE : (h + 1) * SHARE].astype(BF16)
            out_ref[4 * i + h, 0, SHARE:, :] = extra
        return carry

    lax.fori_loop(0, 4, restore_step, 0, unroll=4)


def in_windows(window_order):
    return jnp.pad(
        window_order.reshape(FRAMES, WINDOWS, WINDOW),
        ((0, 0), (0, 0), (0, SLOT - WINDOW)),
        constant_values=-1,
    ).reshape(FRAMES, ROWS // 128, 128)


def attend(f, tokens, order, frame_decay, clip_id, weight, *held):
    fixed = lambda shape, at: pl.BlockSpec(shape, lambda n: at, pipeline_mode=pl.Buffered(1))
    return pl.pallas_call(
        functools.partial(attend_kernel, f),
        grid=(1,),
        in_specs=[
            pl.BlockSpec(memory_space=pltpu.HBM),
            fixed((1, ROWS // 128, 128), (f, 0, 0)),
            fixed((FRAMES, C), (0, 0)),
            pl.BlockSpec(memory_space=pltpu.SMEM),
            pl.BlockSpec(memory_space=pltpu.HBM),
        ]
        + [pl.BlockSpec(memory_space=pltpu.HBM)] * len(held),
        out_specs=fixed((16, 1, SENT, C), (0, f, 0, 0)),
        out_shape=jax.ShapeDtypeStruct((16, FRAMES, SENT, C), BF16),
        scratch_shapes=[
            pltpu.VMEM((TOK, D), BF16),
            pltpu.VMEM((3, D, C), BF16),
            pltpu.VMEM((TOK, D), BF16),
            pltpu.VMEM((TOK, 3 * C), BF16),
            pltpu.VMEM((ROWS, 3 * C), BF16),
            pltpu.VMEM((ROWS, C), BF16),
            pltpu.SemaphoreType.DMA((15,)),
        ],
        input_output_aliases={5: 0} if held else {},
        compiler_params=pltpu.CompilerParams(vmem_limit_bytes=WHOLE),
        cost_estimate=pl.CostEstimate(
            flops=2 * (TOK * D * 3 * C + ROWS * TOK * 3 * C + 4 * ROWS * C * C + ROWS * TOK * C),
            bytes_accessed=TOK * D * 4,
            transcendentals=ROWS * C,
        ),
        name="attend",
    )(tokens, order, frame_decay, clip_id, weight, *held)


def weight_copies(place_ref, weight_refs, held, sems, first, rows):
    c, h = place_ref[1], place_ref[2]
    near, far = lax.rem(h + 3 + 2 * c, 4), lax.rem(h + 1 + 2 * c, 4)
    places = [(c, h), (1 - c, h), (c, near), (1 - c, near), (1 - c, far), (c, far)]
    places += [(c, lax.rem(h + 2, 4)), (1 - c, lax.rem(h + 2, 4))]
    return [
        pltpu.make_async_copy(
            weight_ref.at[first : first + rows, :], held.at[half, index, first : first + rows, :], sems.at[i]
        )
        for i, (weight_ref, (half, index)) in enumerate(zip(weight_refs, places))
    ]


def recur_kernel(
    place_ref, att_ref, x0_ref, x1_ref, x2_ref, x3_ref, *rest
):
    weight_refs = rest[:8]
    residual_ref, state_ref, decay_ref, open_out_ref, last_ref, normed, held, sems = rest[8:]
    x = place_ref[0]
    h = pl.program_id(0)
    count = FRAMES * SHARE

    @pl.when(h == 0)
    def _():
        mix_copies = weight_copies(place_ref, weight_refs, held, sems.at[0], 0, D // 2)
        recur_copies = weight_copies(place_ref, weight_refs, held, sems.at[1], D // 2, 3 * D // 2)
        for one in mix_copies + recur_copies:
            one.start()
        for one in mix_copies:
            one.wait()
        for s, x_ref in enumerate((x0_ref, x1_ref, x2_ref, x3_ref)):
            source = lax.rem(x + (4 - s), 4)
            pieces = []
            for c in range(2):
                for q in range(2):
                    total = None
                    for k in range(4):
                        left = att_ref[4 * source + k, :, :SHARE, :].reshape(count, C)
                        term = dot(left, held[c, k, q * C : (q + 1) * C, :])
                        total = term if total is None else total + term
                    pieces.append(total)
            residual = x_ref[...].reshape(count, D).astype(F32) + jnp.concatenate(pieces, axis=1)
            residual_ref[source] = residual
            normed[source] = scaled(residual).astype(BF16)
        for one in recur_copies:
            one.wait()

    rows = normed[...].reshape(4 * count, D)

    def project(i):
        part = slice((i + 1) * D // 2, (i + 2) * D // 2)
        return dot(rows[:, : D // 2], held[0, h, part, :]) + dot(rows[:, D // 2 :], held[1, h, part, :])

    driven = jax.nn.sigmoid(project(0)) * project(1)
    opening = project(2)
    open_out_ref[0] = opening * jax.nn.sigmoid(opening)
    state = jnp.zeros((SHARE, C), F32)
    first = before = None
    decay = jnp.ones((1, C), F32)
    for f in range(4 * FRAMES):
        extra = att_ref[(f // 2) * 4 + h, f % 2, SHARE:, :].astype(F32)
        retain = jnp.exp(extra[0:1] + extra[1:2] + extra[2:3])
        clip = extra[3:4]
        factor = retain * jnp.where(clip == before, 1.0, 0.0) if f else retain
        first = first if f else clip
        before = clip
        drive = jnp.sqrt(1.0 - retain * retain)
        decay = factor * decay
        state = factor * state + drive * driven[f * SHARE : (f + 1) * SHARE]
        state_ref[0, f * SHARE : (f + 1) * SHARE, :] = state
        decay_ref[0, f : f + 1, :] = decay
    last_ref[0, :SHARE, :] = state.astype(BF16)
    last_ref[0, SHARE:, :] = jnp.broadcast_to(before, (8, C)).astype(BF16)
    decay_ref[0, 8:, :] = jnp.broadcast_to(first, (8, C))


def finish_kernel(place_ref, state_ref, decay_ref, open_ref, incoming_ref, residual_ref, *rest):
    weight_refs = rest[:8]
    out_ref, rows, held, sems = rest[8:]
    n = pl.program_id(0)

    @pl.when(n == 0)
    def _():
        copies = weight_copies(place_ref, weight_refs, held, sems, 2 * D, D // 2)
        for one in copies:
            one.start()
        for k in range(4):
            continues = incoming_ref[k, SHARE:, :].astype(F32) == decay_ref[k, 8:, :]
            incoming = incoming_ref[k, :SHARE, :].astype(F32) * jnp.where(continues, 1.0, 0.0)[:1]
            for f in range(4 * FRAMES):
                piece = slice(f * SHARE, (f + 1) * SHARE)
                state = state_ref[k, piece, :] + decay_ref[k, f : f + 1, :] * incoming
                rows[k, piece, :] = (state * open_ref[k, piece, :]).astype(BF16)
        for one in copies:
            one.wait()

    total = residual_ref[...].reshape(8 * SHARE, C)
    part = pl.ds(pl.multiple_of(2 * D + lax.rem(n, 2) * C, C), C)
    for k in range(4):
        total = total + dot(rows[k], held[n // 2, k, part, :])
    out_ref[...] = total.reshape(4, 1, FRAMES, SHARE, C).astype(BF16)


def place_kernel(in_ref, out_ref, held, sems, out_sems):
    copies = []
    for x in range(4):
        for k in range(4):
            size = STRIDE if k < 3 else SHARE
            i = len(copies)
            through = held.at[i, :, :size, :]
            inward = pltpu.make_async_copy(in_ref.at[x, k, :, :size, :], through, sems.at[i])
            target = out_ref.at[:, x, k * STRIDE : k * STRIDE + size, :]
            copies.append((inward, pltpu.make_async_copy(through, target, out_sems.at[i])))
            inward.start()
    for inward, outward in copies:
        inward.wait()
        outward.start()
    for inward, outward in copies:
        outward.wait()


def per_device(tokens, window_order, clip_id, attend_weight, attend_out, recur_weight, frame_decay, recur_out):
    c, z, x, h = (lax.axis_index(name) for name in ("clip", "z", "x", "head"))

    place = jnp.stack([x, c, h])
    here = pl.BlockSpec(memory_space=pltpu.HBM)
    first, second, *blocks = pl.pallas_call(
        pack_kernel,
        in_specs=[pl.BlockSpec(memory_space=pltpu.SMEM), here, here, here, here],
        out_specs=[here] * 6,
        out_shape=[jax.ShapeDtypeStruct((5 * D // 2, C), BF16)] * 2
        + [jax.ShapeDtypeStruct((FRAMES, SHARE, D), BF16)] * 4,
        scratch_shapes=[
            pltpu.VMEM((2, 5 * D // 2, C), BF16),
            pltpu.VMEM((4, FRAMES, SHARE, D), BF16),
            pltpu.SemaphoreType.DMA((18,)),
            pltpu.SemaphoreType.DMA((18,)),
        ],
        name="pack",
    )(place, tokens.reshape(FRAMES, 4, QUARTER, D), attend_out, recur_weight, recur_out)
    def pinned(value):
        return pltpu.with_memory_space_constraint(value, pltpu.HBM)

    def onward(value):
        pairs = [(i, (i + 1) % 4) for i in range(4)] + [(4 + i, 4 + (i + 3) % 4) for i in range(4)]
        return lax.ppermute(value, ("clip", "head"), pairs)

    def across(value):
        return lax.ppermute(value, "clip", [(0, 1), (1, 0)])

    near_first = onward(first)
    near_second = onward(second)
    moved = [
        lax.ppermute(blocks[s], "x", [(i, (i + s) % 4) for i in range(4)]) if s else blocks[0] for s in range(4)
    ]

    order = in_windows(window_order)
    tokens, attend_weight = pinned(tokens), pinned(attend_weight)
    mixed = attend(0, tokens, order, frame_decay, clip_id, attend_weight)
    mixed, near_first, moved[1], moved[3] = lax.optimization_barrier((mixed, near_first, moved[1], moved[3]))
    far_first = onward(near_first)
    other_first = across(near_first)
    mixed = attend(1, tokens, order, frame_decay, clip_id, attend_weight, mixed)
    mixed, near_second, other_first, *moved = lax.optimization_barrier((mixed, near_second, other_first, *moved))
    other_second = across(near_second)
    far_second = across(far_first)
    weights = (first, second, near_first, near_second, other_first, other_second, far_first, far_second)
    mixed = lax.all_to_all(mixed, ("x", "head"), 0, 0)

    whole = lambda shape: pl.BlockSpec(shape, lambda n: (0,) * len(shape), pipeline_mode=pl.Buffered(1))
    wide = 8 * SHARE
    residual, state, decay, opened, last = pl.pallas_call(
        recur_kernel,
        grid=(4,),
        in_specs=[
            pl.BlockSpec(memory_space=pltpu.SMEM),
            whole((16, FRAMES, SENT, C)),
            whole((FRAMES, SHARE, D)),
            whole((FRAMES, SHARE, D)),
            whole((FRAMES, SHARE, D)),
            whole((FRAMES, SHARE, D)),
            *[here] * 8,
        ],
        out_specs=[
            pl.BlockSpec((4, FRAMES * SHARE, D), lambda n: (0, 0, 0)),
            pl.BlockSpec((1, wide, C), lambda n: (n, 0, 0)),
            pl.BlockSpec((1, 16, C), lambda n: (n, 0, 0)),
            pl.BlockSpec((1, wide, C), lambda n: (n, 0, 0)),
            pl.BlockSpec((1, SENT, C), lambda n: (n, 0, 0)),
        ],
        out_shape=[
            jax.ShapeDtypeStruct((4, FRAMES * SHARE, D), F32),
            jax.ShapeDtypeStruct((4, wide, C), F32),
            jax.ShapeDtypeStruct((4, 16, C), F32),
            jax.ShapeDtypeStruct((4, wide, C), F32),
            jax.ShapeDtypeStruct((4, SENT, C), BF16),
        ],
        scratch_shapes=[
            pltpu.VMEM((4, FRAMES * SHARE, D), BF16),
            pltpu.VMEM((2, 4, 2 * D, C), BF16),
            pltpu.SemaphoreType.DMA((2, 8)),
        ],
        compiler_params=pltpu.CompilerParams(vmem_limit_bytes=LIMIT),
        name="recur",
    )(place, mixed, *map(pinned, moved), *map(pinned, weights))

    incoming = lax.ppermute(last, "z", [(i, i + 1) for i in range(3)])

    result = pl.pallas_call(
        finish_kernel,
        grid=(4,),
        in_specs=[
            pl.BlockSpec(memory_space=pltpu.SMEM),
            whole((4, wide, C)),
            whole((4, 16, C)),
            whole((4, wide, C)),
            whole((4, SENT, C)),
            pl.BlockSpec((4, FRAMES * SHARE, C), lambda n: (0, 0, n)),
            *[here] * 8,
        ],
        out_specs=pl.BlockSpec((4, 1, FRAMES, SHARE, C), lambda n: (0, n, 0, 0, 0)),
        out_shape=jax.ShapeDtypeStruct((4, 4, FRAMES, SHARE, C), BF16),
        scratch_shapes=[
            pltpu.VMEM((4, wide, C), BF16),
            pltpu.VMEM((2, 4, 5 * D // 2, C), BF16),
            pltpu.SemaphoreType.DMA((8,)),
        ],
        compiler_params=pltpu.CompilerParams(vmem_limit_bytes=LIMIT),
        name="finish",
    )(place, state, decay, opened, incoming, residual, *map(pinned, weights))

    result = lax.all_to_all(result.reshape(16, FRAMES, SHARE, C), ("x", "head"), 0, 0)
    placed = pl.pallas_call(
        place_kernel,
        in_specs=[here],
        out_specs=here,
        out_shape=jax.ShapeDtypeStruct((FRAMES, 4, QUARTER, C), BF16),
        scratch_shapes=[
            pltpu.VMEM((16, FRAMES, SHARE, C), BF16),
            pltpu.SemaphoreType.DMA((16,)),
            pltpu.SemaphoreType.DMA((16,)),
        ],
        name="place",
    )(result.reshape(4, 4, FRAMES, SHARE, C))
    return placed.reshape(FRAMES, TOK, C)


def solution(mesh):
    split = Mesh(mesh.devices.reshape(2, 4, 4, 4), ("clip", "z", "x", "head"))
    frames = ("clip", "z", "x")
    return jax.shard_map(
        per_device,
        mesh=split,
        in_specs=(
            P(frames, None, None),
            P(frames, None),
            P(frames),
            P(None, None, "head"),
            P("head", None),
            P(None, None, "head"),
            P(frames, "head"),
            P("head", None),
        ),
        out_specs=P(frames, None, "head"),
        check_vma=False,
    )
```
